256 devices in a mesh: gx: 2 (over core), gy: 16 (over y, x), gz: 8 (over z).
Axes of the slice: x: 4, y: 4, z: 8, core: 2. Of those that a mesh axis runs over, the one named last changes fastest.
Arguments:
- tokens: bfloat16 [2048, 8192], P('gy', ('gz', 'gx')), may hold values from -6 to 6
- gate_weight: bfloat16 [8192, 8192], P('gz', ('gx', 'gy')), may hold values from -0.0625 to 0.0625
- up_weight: bfloat16 [8192, 8192], P('gz', ('gx', 'gy')), may hold values from -0.0625 to 0.0625
- down_weight: bfloat16 [8192, 8192], P('gz', ('gx', 'gy')), may hold values from -0.0625 to 0.0625
- out_grad: bfloat16 [2048, 8192], P('gy', ('gz', 'gx')), may hold values from -6 to 6
Outputs:
- output: bfloat16 [2048, 8192], P('gy', ('gz', 'gx'))
- tokens_grad: bfloat16 [2048, 8192], P('gy', ('gz', 'gx'))
- gate_grad_w: float32 [8192, 8192], P('gz', ('gx', 'gy'))
- up_grad_w: float32 [8192, 8192], P('gz', ('gx', 'gy'))
- down_grad_w: float32 [8192, 8192], P('gz', ('gx', 'gy'))
The draws below stay inside these ranges and needn't reach their ends.
All inputs are finite; a program needn't handle non-finite values.
Results may differ from the reference program's by a relative error of at most 0.023.
Values may be sent and summed in bfloat16 or wider, within the bound.
A program may use at most 128 MiB of HBM per device.

```python
import jax
import jax.numpy as jnp
from jax import lax

D = 8192
FF = 8192
TOKENS = 2048
N_GX = 2
N_GZ = 8


def level_of(key, dims, split, smallest, largest):
    factor_of, own = 1.0, jax.random.fold_in(key, 6)
    for axis_at, parts in split:
        heights = jnp.exp(jax.random.uniform(jax.random.fold_in(own, axis_at), (parts,), jnp.float32, smallest / len(split), largest / len(split)))
        factor_of = factor_of * jnp.repeat(heights, dims[axis_at] // parts).reshape([-1 if axis == axis_at else 1 for axis in range(len(dims))])
    return factor_of


def normal_values(stream_key, dims, spread, limit, pieces=(), kind=jnp.bfloat16):
    gain = level_of(stream_key, dims, pieces, -0.22, 0.18) if pieces else 1.0
    array = jax.random.normal(stream_key, dims, jnp.float32) * spread * gain
    return jnp.minimum(jnp.maximum(array, -limit), limit).astype(kind)


def setup_inputs(seed: int = 0) -> dict:
    seeds = jax.random.split(jax.random.key(seed), 6)
    tokens = normal_values(seeds[0], (TOKENS, D), 1.0, 6.0, ((0, 16), (1, 16)))
    gate_weight = normal_values(seeds[1], (D, FF), D ** -0.5, 0.0625, ((0, 8), (1, 32)))
    up_weight = normal_values(seeds[2], (D, FF), D ** -0.5, 0.0625, ((0, 8), (1, 32)))
    down_weight = normal_values(seeds[3], (D, FF), FF ** -0.5, 0.0625, ((0, 8), (1, 32)))
    out_grad = normal_values(seeds[4], (TOKENS, D), 1.0, 6.0, ((0, 16), (1, 16)))
    return dict(tokens=tokens, gate_weight=gate_weight, up_weight=up_weight, down_weight=down_weight, out_grad=out_grad)


def rounded(value):
    return lax.optimization_barrier(value.astype(jnp.bfloat16)).astype(jnp.float32)


def dot_last(left, right):
    return lax.dot_general(left, right, (((1,), (1,)), ((), ())), preferred_element_type=jnp.float32)


def reference(tokens, gate_weight, up_weight, down_weight, out_grad):
    feat_block = D // N_GZ
    unit_block = FF // N_GX
    gate_value = jnp.zeros((TOKENS, FF), jnp.float32)
    up_value = jnp.zeros((TOKENS, FF), jnp.float32)
    hidden_grad = jnp.zeros((TOKENS, FF), jnp.float32)
    for block_index in range(N_GZ):
        low = block_index * feat_block
        x_part = tokens[:, low:low + feat_block]
        gate_value = gate_value + rounded(jnp.dot(x_part, gate_weight[low:low + feat_block], preferred_element_type=jnp.float32))
        up_value = up_value + rounded(jnp.dot(x_part, up_weight[low:low + feat_block], preferred_element_type=jnp.float32))
        grad_part = out_grad[:, low:low + feat_block]
        hidden_grad = hidden_grad + rounded(jnp.dot(grad_part, down_weight[low:low + feat_block], preferred_element_type=jnp.float32))
    activated = jax.nn.silu(gate_value)
    hidden = (activated * up_value).astype(jnp.bfloat16)
    sigmoid_gate = jax.nn.sigmoid(gate_value)
    gate_grad = (hidden_grad * up_value * sigmoid_gate * (1.0 + gate_value * (1.0 - sigmoid_gate))).astype(jnp.bfloat16)
    up_grad = (hidden_grad * activated).astype(jnp.bfloat16)
    out_sum = jnp.zeros((TOKENS, D), jnp.float32)
    in_sum = jnp.zeros((TOKENS, D), jnp.float32)
    for block_index in range(N_GX):
        low = block_index * unit_block
        high = low + unit_block
        out_sum = out_sum + rounded(dot_last(hidden[:, low:high], down_weight[:, low:high]))
        term = dot_last(gate_grad[:, low:high], gate_weight[:, low:high]) + dot_last(up_grad[:, low:high], up_weight[:, low:high])
        in_sum = in_sum + rounded(term)
    output = out_sum.astype(jnp.bfloat16)
    tokens_grad = in_sum.astype(jnp.bfloat16)
    gate_grad_w = jnp.dot(tokens.T, gate_grad, preferred_element_type=jnp.float32)
    up_grad_w = jnp.dot(tokens.T, up_grad, preferred_element_type=jnp.float32)
    down_grad_w = jnp.dot(out_grad.T, hidden, preferred_element_type=jnp.float32)
    return (output, tokens_grad, gate_grad_w, up_grad_w, down_grad_w)
```

```python
import jax
import jax.numpy as jnp
from jax import lax
from jax.sharding import PartitionSpec as P


def dot_last(left, right):
    return lax.dot_general(
        left, right, (((1,), (1,)), ((), ())), preferred_element_type=jnp.float32
    )


def dot_first(left, right):
    return lax.dot_general(
        left, right, (((0,), (0,)), ((), ())), preferred_element_type=jnp.float32
    )


def per_device(tokens, gate_weight, up_weight, down_weight, out_grad):
    x_half = lax.all_gather(tokens, "gy", axis=0, tiled=True)
    g_half = lax.all_gather(out_grad, "gy", axis=0, tiled=True)
    x_all = lax.all_gather(x_half, "gx", axis=1, tiled=True)
    g_all = lax.all_gather(g_half, "gx", axis=1, tiled=True)
    width = gate_weight.shape[1]
    both_weight = jnp.concatenate([gate_weight, up_weight], axis=1)
    both_part = jnp.dot(x_all, both_weight, preferred_element_type=jnp.float32)
    both_values = lax.psum_scatter(
        both_part.astype(jnp.bfloat16), "gz", scatter_dimension=0, tiled=True
    ).astype(jnp.float32)
    hidden_grad = lax.psum_scatter(
        jnp.dot(g_all, down_weight, preferred_element_type=jnp.float32).astype(jnp.bfloat16),
        "gz",
        scatter_dimension=0,
        tiled=True,
    ).astype(jnp.float32)
    gate_value = both_values[:, :width]
    up_value = both_values[:, width:]
    sigmoid_gate = jax.nn.sigmoid(gate_value)
    activated = gate_value * sigmoid_gate
    hidden = (activated * up_value).astype(jnp.bfloat16)
    gate_grad = (
        hidden_grad * up_value * sigmoid_gate * (1.0 + gate_value * (1.0 - sigmoid_gate))
    ).astype(jnp.bfloat16)
    up_grad = (hidden_grad * activated).astype(jnp.bfloat16)
    hidden_all = lax.all_gather(hidden, "gz", axis=0, tiled=True)
    grads_all = lax.all_gather(
        jnp.concatenate([gate_grad, up_grad], axis=1), "gz", axis=0, tiled=True
    )

    def scatter(part):
        pair = lax.psum_scatter(
            part.astype(jnp.bfloat16), "gx", scatter_dimension=1, tiled=True
        )
        return lax.psum_scatter(pair, "gy", scatter_dimension=0, tiled=True)

    output = scatter(dot_last(hidden_all, down_weight))
    tokens_grad = scatter(dot_last(grads_all, both_weight))
    both_grad_w = dot_first(x_all, grads_all)
    down_grad_w = dot_first(g_all, hidden_all)
    return (output, tokens_grad, both_grad_w[:, :width], both_grad_w[:, width:], down_grad_w)


def solution(mesh):
    return jax.shard_map(
        per_device,
        mesh=mesh,
        in_specs=(
            P("gy", ("gz", "gx")),
            P("gz", ("gx", "gy")),
            P("gz", ("gx", "gy")),
            P("gz", ("gx", "gy")),
            P("gy", ("gz", "gx")),
        ),
        out_specs=(
            P("gy", ("gz", "gx")),
            P("gy", ("gz", "gx")),
            P("gz", ("gx", "gy")),
            P("gz", ("gx", "gy")),
            P("gz", ("gx", "gy")),
        ),
        check_vma=False,
    )
```

```python
import jax
import jax.numpy as jnp
from jax import lax
from jax.experimental import pallas as pl
from jax.experimental.pallas import tpu as pltpu
from jax.sharding import PartitionSpec as P

MESH = pl.DeviceIdType.MESH
F32 = jnp.float32
BF16 = jnp.bfloat16


def dot_plain(left, right):
    return jnp.dot(left, right, preferred_element_type=F32)


def dot_last(left, right):
    return lax.dot_general(left, right, (((1,), (1,)), ((), ())), preferred_element_type=F32)


def dot_first(left, right):
    return lax.dot_general(left, right, (((0,), (0,)), ((), ())), preferred_element_type=F32)


def kernel(
    tok, wg, wu, wd, grd,
    out_ref, tg_ref, dg_ref, du_ref, dd_ref,
    act, w, rs_send, rs_recv, hall, gu, q, ps, pr, sa, ra, sb, rb, sc, rc,
    local_sem, s1, r1, s2, r2, s3, r3, sp, rp, zs, zr, as_, ar, pss, prs,
    sas, ras, sbs, rbs, scs, rcs,
):
    c = lax.axis_index("gx")
    gy = lax.axis_index("gy")
    z = lax.axis_index("gz")
    y, x = gy // 4, gy % 4
    f = x * (1 - c) + y * c
    s = y * (1 - c) + x * c
    fm, sm = 1 + 3 * c, 4 - 3 * c
    sg = 1 - 2 * c
    partner = (1 - c, gy, z)

    def gy_of(f_, s_):
        return ((f_ + 8) % 4) * fm + ((s_ + 8) % 4) * sm

    def at_fs(f_, s_):
        return (c, gy_of(f_, s_), z)

    def mod8(k):
        return (k + 16) % 8

    def at_z(k):
        return (c, gy, mod8(z + k))

    def rows_of(block):
        return pl.ds(pl.multiple_of(block * 128, 128), 128)

    def zrows(block):
        return pl.ds(pl.multiple_of(block * 256, 256), 256)

    sends = []

    def send(src, dst, ss, rs, device):
        copy = pltpu.make_async_remote_copy(
            src_ref=src, dst_ref=dst, send_sem=ss, recv_sem=rs,
            device_id=device, device_id_type=MESH,
        )
        copy.start()
        sends.append(copy)

    def recv(dst, ss, rs):
        pltpu.make_async_remote_copy(
            src_ref=dst, dst_ref=dst, send_sem=ss, recv_sem=rs,
            device_id=partner, device_id_type=MESH,
        ).wait_recv()

    barrier = pltpu.get_barrier_semaphore()
    peers = [
        at_fs(f + 1, s), at_fs(f + 2, s), at_fs(f + 3, s), at_fs(f, s + 1), at_fs(f, s + 3),
        at_z(1), at_z(-1), partner,
    ]
    for peer in peers:
        pl.semaphore_signal(barrier, inc=1, device_id=peer, device_id_type=MESH)

    own = [(tok, 0), (grd, 1)]
    locals_ = [
        pltpu.make_async_copy(wg, w.at[0], local_sem.at[0]),
        pltpu.make_async_copy(wu, w.at[1], local_sem.at[1]),
        pltpu.make_async_copy(wd, w.at[2], local_sem.at[2]),
        pltpu.make_async_copy(tok, act.at[0, c, rows_of(gy)], local_sem.at[3]),
        pltpu.make_async_copy(grd, act.at[1, c, rows_of(gy)], local_sem.at[4]),
    ]
    for copy in locals_:
        copy.start()
    pl.semaphore_wait(barrier, len(peers))

    def block(k, t):
        return gy_of(f - k, s + t)

    def act_block(a, k, t):
        return act.at[a, c, rows_of(block(k, t))]

    def to_partner(a, k, t, src=None):
        ref = act_block(a, k, t)
        send(ref if src is None else src, ref, sp.at[a, 4 * t + k], rp.at[a, 4 * t + k], partner)

    def gather_own(a):
        src = own[a][0]
        ref = act_block(a, 0, 0)
        for k in (1, 3, 2):
            send(src, ref, s1.at[a, k], r1.at[a, k], at_fs(f + k, s))
        send(src, ref, s2.at[a, 0, 0], r2.at[a, 0, 0], at_fs(f, s + 1))
        send(src, ref, s2.at[a, 1, 0], r2.at[a, 1, 0], at_fs(f, s + 3))
        to_partner(a, 0, 0, src)

    def gather_row(a):
        for k in (1, 3, 2):
            ref = act_block(a, k, 0)
            recv(ref, s1.at[a, k], r1.at[a, k])
            send(ref, ref, s2.at[a, 0, k], r2.at[a, 0, k], at_fs(f, s + 1))
            send(ref, ref, s2.at[a, 1, k], r2.at[a, 1, k], at_fs(f, s + 3))
            to_partner(a, k, 0)

    def gather_near(a):
        for k in (0, 1, 3, 2):
            for way, t in ((0, 3), (1, 1)):
                ref = act_block(a, k, t)
                recv(ref, s2.at[a, way, k], r2.at[a, way, k])
                if way == 0 and k < 2:
                    send(ref, ref, s3.at[a, k], r3.at[a, k], at_fs(f, s + 1))
                if way == 1 and k >= 2:
                    send(ref, ref, s3.at[a, k], r3.at[a, k], at_fs(f, s + 3))
                to_partner(a, k, t)

    def gather_far(a):
        for k in (0, 3, 1, 2):
            ref = act_block(a, k, 2)
            recv(ref, s3.at[a, k], r3.at[a, k])
            to_partner(a, k, 2)

    def gather_end(a):
        for t in (0, 3, 1, 2):
            for k in range(4):
                ref = act.at[a, 1 - c, rows_of(gy_of(f + t, s - k))]
                recv(ref, sp.at[a, 4 * t + k], rp.at[a, 4 * t + k])
        locals_[3 + a].wait()

    def part(a, d):
        rows = zrows(d)
        source = 0 if a < 2 else 1
        return dot_plain(act[source, 0, rows, :], w[a, 0:512, :]) + dot_plain(
            act[source, 1, rows, :], w[a, 512:1024, :]
        )

    def sum_step(arrays, j):
        for a in arrays:
            for base, last, d, to in (
                (0, 4, z - sg * (4 - j), -sg), (4, 3, z + sg * (3 - j), sg)
            ):
                if j >= last:
                    continue
                value = part(a, mod8(d))
                if j > 0:
                    recv(rs_recv.at[a, base + j - 1], zs.at[a, base + j - 1], zr.at[a, base + j - 1])
                    value = value + rs_recv[a, base + j - 1].astype(F32)
                rs_send[a, base + j] = value.astype(BF16)
                send(
                    rs_send.at[a, base + j], rs_recv.at[a, base + j],
                    zs.at[a, base + j], zr.at[a, base + j], at_z(to),
                )

    def sum_end(a):
        value = part(a, z)
        for slot in (3, 6):
            recv(rs_recv.at[a, slot], zs.at[a, slot], zr.at[a, slot])
            value = value + rs_recv[a, slot].astype(F32)
        return value

    def zrecv(t, slot, b):
        recv(hall.at[t, zrows(b)], as_.at[t, slot], ar.at[t, slot])

    def zgather(t, j):
        for base, last, way in ((0, 4, sg), (4, 3, -sg)):
            b = mod8(z + way * j)
            if j > 0 and j <= last:
                zrecv(t, base + j - 1, b)
            if j < last:
                ref = hall.at[t, zrows(b)]
                send(ref, ref, as_.at[t, base + j], ar.at[t, base + j], at_z(-way))

    def product(o, b, half):
        rows = zrows(b)
        cols = pl.ds(pl.multiple_of(half * 512, 512), 512)
        if o == 0:
            return dot_last(hall[0, rows, :], w[2, cols, :])
        return dot_last(hall[1, rows, :], w[0, cols, :]) + dot_last(hall[2, rows, :], w[1, cols, :])

    def out_block(o, b):
        rows = zrows(b)
        ps[o, rows, :] = product(o, b, 1 - c).astype(BF16)
        send(ps.at[o, rows], pr.at[o, rows], pss.at[o, b], prs.at[o, b], partner)
        q[o, rows, :] = product(o, b, c)

    def out_pair_end(o):
        for b in range(8):
            recv(pr.at[o, zrows(b)], pss.at[o, b], prs.at[o, b])

    def chip_sum(o, k, t):
        rows = rows_of(gy_of(f + k, s + t))
        return q[o, rows, :] + pr[o, rows, :].astype(F32)

    def stage_a(o):
        for k in (0, 2, 1, 3):
            sa[o, k] = chip_sum(o, k, 2).astype(BF16)
            send(sa.at[o, k], ra.at[o, k], sas.at[o, k], ras.at[o, k], at_fs(f, s + (1 if k < 2 else 3)))

    def stage_b(o):
        for k in (2, 3, 0, 1):
            for way, t, kk in ((0, 1, k), (1, 3, (k + 2) % 4)):
                value = chip_sum(o, kk, t)
                if (way == 0) == (kk < 2):
                    recv(ra.at[o, kk], sas.at[o, kk], ras.at[o, kk])
                    value = value + ra[o, kk].astype(F32)
                sb[o, 4 * way + kk] = value.astype(BF16)
                send(
                    sb.at[o, 4 * way + kk], rb.at[o, 4 * way + kk],
                    sbs.at[o, 4 * way + kk], rbs.at[o, 4 * way + kk], at_fs(f, s + t),
                )

    def stage_c(o):
        for k in (2, 3, 1, 0):
            value = chip_sum(o, k, 0)
            for way in range(2):
                slot = 4 * way + k
                recv(rb.at[o, slot], sbs.at[o, slot], rbs.at[o, slot])
                value = value + rb[o, slot].astype(F32)
            if k > 0:
                sc[o, k] = value.astype(BF16)
                send(sc.at[o, k], rc.at[o, k], scs.at[o, k], rcs.at[o, k], at_fs(f + k, s))
            else:
                q[o, rows_of(gy), :] = value

    def stage_d(o, ref):
        value = q[o, rows_of(gy), :]
        for k in (1, 3, 2):
            recv(rc.at[o, k], scs.at[o, k], rcs.at[o, k])
            value = value + rc[o, k].astype(F32)
        ref[...] = value.astype(BF16)

    def weight_grad(ref, a, t):
        for half in range(2):
            ref[half * 512:(half + 1) * 512, :] = dot_first(act[a, half], hall[t])

    gather_own(0)
    gather_row(0)
    gather_own(1)
    gather_near(0)
    gather_row(1)
    gather_far(0)
    for copy in locals_[:3]:
        copy.wait()
    gather_end(0)
    sum_step((0, 1), 0)
    gather_near(1)
    sum_step((0, 1), 1)
    gather_far(1)
    sum_step((0, 1), 2)
    gather_end(1)
    sum_step((2,), 0)
    sum_step((0, 1), 3)
    sum_step((2,), 1)
    gate = sum_end(0)
    up = sum_end(1)
    gu[0] = gate
    gu[1] = up
    sigmoid = jax.nn.sigmoid(gate)
    hall[0, zrows(z), :] = (gate * sigmoid * up).astype(BF16)
    zgather(0, 0)
    sum_step((2,), 2)
    out_block(0, z)
    sum_step((2,), 3)
    zgather(0, 1)
    out_block(0, mod8(z + 1))
    out_block(0, mod8(z - 1))
    hidden_grad = sum_end(2)
    gate = gu[0]
    up = gu[1]
    sigmoid = jax.nn.sigmoid(gate)
    hall[1, zrows(z), :] = (
        hidden_grad * up * sigmoid * (1.0 + gate * (1.0 - sigmoid))
    ).astype(BF16)
    zgather(1, 0)
    hall[2, zrows(z), :] = (hidden_grad * (gate * sigmoid)).astype(BF16)
    zgather(2, 0)
    zgather(0, 2)
    out_block(0, mod8(z + 2))
    out_block(0, mod8(z - 2))
    zgather(0, 3)
    out_block(0, mod8(z + 3))
    zgather(1, 1)
    zgather(2, 1)
    out_block(0, mod8(z - 3))
    zrecv(0, 3, mod8(z + 4 * sg))
    out_block(0, mod8(z + 4))
    out_block(1, z)
    out_pair_end(0)
    stage_a(0)
    out_block(1, mod8(z + 1))
    out_block(1, mod8(z - 1))
    zgather(1, 2)
    zgather(2, 2)
    stage_b(0)
    out_block(1, mod8(z + 2))
    out_block(1, mod8(z - 2))
    zgather(1, 3)
    zgather(2, 3)
    stage_c(0)
    out_block(1, mod8(z + 3))
    out_block(1, mod8(z - 3))
    weight_grad(dd_ref, 1, 0)
    stage_d(0, out_ref)
    zrecv(1, 3, mod8(z + 4 * sg))
    zrecv(2, 3, mod8(z + 4 * sg))
    out_block(1, mod8(z + 4))
    out_pair_end(1)
    stage_a(1)
    stage_b(1)
    weight_grad(dg_ref, 0, 1)
    stage_c(1)
    weight_grad(du_ref, 0, 2)
    stage_d(1, tg_ref)
    for copy in sends:
        copy.wait_send()


def per_device(tokens, gate_weight, up_weight, down_weight, out_grad):
    dma = pltpu.SemaphoreType.DMA
    vmem = pltpu.VMEM
    return pl.pallas_call(
        kernel,
        out_shape=(
            jax.ShapeDtypeStruct((128, 512), BF16),
            jax.ShapeDtypeStruct((128, 512), BF16),
            jax.ShapeDtypeStruct((1024, 256), F32),
            jax.ShapeDtypeStruct((1024, 256), F32),
            jax.ShapeDtypeStruct((1024, 256), F32),
        ),
        in_specs=[pl.BlockSpec(memory_space=pl.ANY)] * 5,
        out_specs=tuple([pl.BlockSpec(memory_space=pltpu.VMEM)] * 5),
        scratch_shapes=[
            vmem((2, 2, 2048, 512), BF16),
            vmem((3, 1024, 256), BF16),
            vmem((3, 7, 256, 256), BF16),
            vmem((3, 7, 256, 256), BF16),
            vmem((3, 2048, 256), BF16),
            vmem((2, 256, 256), F32),
            vmem((2, 2048, 512), F32),
            vmem((2, 2048, 512), BF16),
            vmem((2, 2048, 512), BF16),
            vmem((2, 4, 128, 512), BF16),
            vmem((2, 4, 128, 512), BF16),
            vmem((2, 8, 128, 512), BF16),
            vmem((2, 8, 128, 512), BF16),
            vmem((2, 4, 128, 512), BF16),
            vmem((2, 4, 128, 512), BF16),
            dma((5,)),
            dma((2, 4)), dma((2, 4)),
            dma((2, 2, 4)), dma((2, 2, 4)),
            dma((2, 4)), dma((2, 4)),
            dma((2, 16)), dma((2, 16)),
            dma((3, 7)), dma((3, 7)),
            dma((3, 7)), dma((3, 7)),
            dma((2, 8)), dma((2, 8)),
            dma((2, 4)), dma((2, 4)),
            dma((2, 8)), dma((2, 8)),
            dma((2, 4)), dma((2, 4)),
        ],
        compiler_params=pltpu.CompilerParams(
            collective_id=0, has_side_effects=True, vmem_limit_bytes=60 * 1024 * 1024
        ),
        name="slab",
    )(tokens, gate_weight, up_weight, down_weight, out_grad)


def solution(mesh):
    return jax.shard_map(
        per_device,
        mesh=mesh,
        in_specs=(
            P("gy", ("gz", "gx")),
            P("gz", ("gx", "gy")),
            P("gz", ("gx", "gy")),
            P("gz", ("gx", "gy")),
            P("gy", ("gz", "gx")),
        ),
        out_specs=(
            P("gy", ("gz", "gx")),
            P("gy", ("gz", "gx")),
            P("gz", ("gx", "gy")),
            P("gz", ("gx", "gy")),
            P("gz", ("gx", "gy")),
        ),
        check_vma=False,
    )
```

```python
import jax
import jax.numpy as jnp
from jax import lax
from jax.experimental import pallas as pl
from jax.experimental.pallas import tpu as pltpu
from jax.sharding import PartitionSpec as P

MESH = pl.DeviceIdType.MESH
F32 = jnp.float32
BF16 = jnp.bfloat16


def dot_plain(left, right):
    return jnp.dot(left, right, preferred_element_type=F32)


def dot_last(left, right):
    return lax.dot_general(left, right, (((1,), (1,)), ((), ())), preferred_element_type=F32)


def dot_first(left, right):
    return lax.dot_general(left, right, (((0,), (0,)), ((), ())), preferred_element_type=F32)


SIZES = (64, 64)
STARTS = tuple(sum(SIZES[:r]) for r in range(len(SIZES)))
ROUNDS = len(SIZES)

ORDER = (
    (0, 0, 0), (16,), (1, 0, 0, 3), (2, 0, 0, 1, 0), (1, 0, 0, 1), (2, 0, 0, 0, 0), (2, 0, 0, 1, 3),
    (1, 0, 0, 2), (0, 0, 1), (2, 0, 0, 0, 3), (2, 0, 0, 1, 1), (2, 0, 0, 0, 1), (3, 0, 0, 0), (3, 0, 0, 3),
    (1, 0, 1, 3), (2, 0, 0, 1, 2), (2, 0, 0, 0, 2), (1, 0, 1, 1), (2, 0, 1, 1, 0), (2, 0, 1, 0, 0),
    (2, 0, 1, 1, 3), (3, 0, 0, 1), (1, 0, 1, 2), (0, 1, 0), (3, 0, 0, 2), (2, 0, 1, 0, 3), (2, 0, 1, 1, 1),
    (2, 0, 1, 0, 1), (4, 0, 0), (5, 0, 0, 0, 0), (5, 0, 0, 0, 1), (5, 1, 0, 0, 0), (3, 0, 1, 0), (3, 0, 1, 3),
    (5, 1, 0, 0, 1), (1, 1, 0, 3), (2, 0, 1, 1, 2), (1, 1, 0, 1), (2, 0, 1, 0, 2), (2, 1, 0, 1, 0),
    (5, 0, 0, 1, 0), (2, 1, 0, 0, 0), (5, 0, 0, 1, 1), (2, 1, 0, 1, 3), (1, 1, 0, 2), (0, 1, 1), (3, 0, 1, 1),
    (5, 1, 0, 1, 0), (3, 0, 1, 2), (5, 1, 0, 1, 1), (2, 1, 0, 0, 3), (2, 1, 0, 1, 1), (5, 0, 0, 2, 0),
    (4, 0, 1), (5, 0, 1, 0, 1), (5, 0, 1, 0, 0), (5, 0, 0, 2, 1), (5, 1, 1, 0, 1), (5, 1, 1, 0, 0),
    (2, 1, 0, 0, 1), (3, 1, 0, 3), (3, 1, 0, 0), (5, 1, 0, 2, 0), (2, 1, 0, 1, 2), (1, 1, 1, 3),
    (5, 1, 0, 2, 1), (2, 1, 0, 0, 2), (1, 1, 1, 1), (2, 1, 1, 1, 0), (5, 0, 0, 3, 0), (2, 1, 1, 0, 0),
    (5, 0, 1, 1, 1), (5, 0, 1, 1, 0), (1, 1, 1, 2), (3, 1, 0, 1), (3, 1, 0, 2), (2, 1, 1, 1, 3),
    (2, 1, 1, 0, 3), (5, 1, 1, 1, 0), (2, 1, 1, 1, 1), (4, 1, 0), (5, 2, 0, 0, 1), (2, 1, 1, 0, 1),
    (5, 2, 0, 0, 0), (5, 1, 1, 1, 1), (3, 1, 1, 0), (5, 1, 0, 3, 0), (2, 1, 1, 1, 2), (2, 1, 1, 0, 2),
    (3, 1, 1, 3), (3, 1, 1, 1), (5, 0, 1, 2, 1), (5, 0, 1, 2, 0), (3, 1, 1, 2), (5, 2, 0, 1, 1),
    (5, 1, 1, 2, 0), (4, 1, 1), (5, 2, 1, 0, 1), (5, 2, 1, 0, 0), (5, 1, 1, 2, 1), (5, 2, 0, 1, 0), (6, 0),
    (9, 0, 0, 0, 0), (5, 2, 0, 2, 1), (5, 0, 1, 3, 0), (5, 2, 1, 1, 1), (5, 1, 1, 3, 0), (5, 2, 1, 1, 0),
    (8, 0, 0, 1, 1), (9, 0, 0, 1, 1), (5, 2, 0, 2, 0), (8, 0, 0, 1, 0), (9, 0, 0, 1, 0), (5, 2, 1, 2, 1),
    (8, 0, 0, 2, 1), (9, 0, 0, 2, 1), (6, 1), (9, 0, 1, 0, 0), (5, 2, 1, 2, 0), (5, 2, 0, 3, 0),
    (8, 0, 0, 3, 1), (9, 0, 0, 3, 1), (8, 0, 0, 2, 0), (9, 0, 0, 2, 0), (8, 0, 1, 1, 1), (9, 0, 1, 1, 1),
    (8, 0, 1, 1, 0), (9, 0, 1, 1, 0), (5, 2, 1, 3, 0), (7, 0), (9, 1, 0, 0, 0), (8, 0, 0, 3, 0),
    (9, 0, 0, 3, 0), (8, 0, 1, 2, 1), (9, 0, 1, 2, 1), (8, 0, 1, 2, 0), (9, 0, 1, 2, 0), (7, 1),
    (9, 1, 1, 0, 0), (8, 1, 0, 1, 1), (8, 1, 0, 1, 0), (8, 2, 0, 1, 1), (9, 1, 0, 1, 1), (8, 2, 0, 1, 0),
    (9, 1, 0, 1, 0), (8, 0, 1, 3, 1), (9, 0, 1, 3, 1), (8, 0, 0, 4, 0), (9, 0, 0, 4, 0), (8, 1, 1, 1, 1),
    (8, 0, 1, 3, 0), (9, 0, 1, 3, 0), (10, 0, 0), (11, 0, 0, 0), (11, 0, 0, 2), (11, 0, 0, 1), (11, 0, 0, 3),
    (12, 0, 0, 1, 0), (12, 0, 0, 1, 1), (12, 0, 0, 0, 2), (12, 0, 0, 0, 3), (8, 2, 1, 1, 1), (9, 1, 1, 1, 1),
    (8, 1, 1, 1, 0), (8, 1, 0, 2, 1), (8, 2, 1, 1, 0), (9, 1, 1, 1, 0), (12, 0, 0, 0, 0), (12, 0, 0, 1, 2),
    (12, 0, 0, 0, 1), (12, 0, 0, 1, 3), (8, 2, 0, 2, 1), (9, 1, 0, 2, 1), (8, 1, 0, 2, 0), (8, 1, 1, 2, 1),
    (8, 2, 0, 2, 0), (9, 1, 0, 2, 0), (13, 0, 0, 2), (13, 0, 0, 0), (13, 0, 0, 1), (8, 2, 1, 2, 1),
    (9, 1, 1, 2, 1), (13, 0, 0, 3), (8, 0, 1, 4, 0), (9, 0, 1, 4, 0), (15, 2), (8, 1, 0, 3, 1),
    (8, 1, 1, 2, 0), (10, 0, 1), (11, 0, 1, 0), (11, 0, 1, 2), (11, 0, 1, 1), (11, 0, 1, 3), (12, 0, 1, 1, 1),
    (12, 0, 1, 1, 0), (8, 2, 0, 3, 1), (12, 0, 1, 0, 3), (12, 0, 1, 0, 2), (9, 1, 0, 3, 1), (8, 2, 1, 2, 0),
    (9, 1, 1, 2, 0), (8, 1, 1, 3, 1), (14, 0, 0), (8, 1, 0, 3, 0), (12, 0, 1, 0, 0), (12, 0, 1, 1, 2),
    (8, 2, 1, 3, 1), (9, 1, 1, 3, 1), (8, 2, 0, 3, 0), (9, 1, 0, 3, 0), (12, 0, 1, 1, 3), (8, 1, 1, 3, 0),
    (12, 0, 1, 0, 1), (8, 2, 1, 3, 0), (9, 1, 1, 3, 0), (8, 1, 0, 4, 0), (13, 0, 1, 0), (13, 0, 1, 2),
    (8, 2, 0, 4, 0), (9, 1, 0, 4, 0), (13, 0, 1, 3), (8, 1, 1, 4, 0), (13, 0, 1, 1), (8, 2, 1, 4, 0),
    (9, 1, 1, 4, 0), (10, 1, 0), (11, 1, 0, 1), (11, 1, 0, 3), (11, 1, 0, 0), (11, 1, 0, 2), (12, 1, 0, 0, 2),
    (12, 1, 0, 1, 1), (12, 1, 0, 1, 0), (12, 1, 0, 0, 3), (10, 1, 1), (11, 1, 1, 1), (11, 1, 1, 3),
    (11, 1, 1, 0), (11, 1, 1, 2), (12, 1, 1, 1, 1), (12, 1, 1, 1, 0), (12, 1, 1, 0, 2), (12, 1, 1, 0, 3),
    (14, 0, 1), (12, 1, 0, 1, 3), (12, 1, 0, 0, 1), (12, 1, 0, 1, 2), (12, 1, 0, 0, 0), (12, 1, 1, 1, 3),
    (12, 1, 1, 0, 1), (12, 1, 1, 1, 2), (12, 1, 1, 0, 0), (15, 0), (15, 1), (13, 1, 0, 1), (13, 1, 0, 3),
    (13, 1, 0, 2), (13, 1, 0, 0), (13, 1, 1, 3), (13, 1, 1, 1), (13, 1, 1, 2), (13, 1, 1, 0), (14, 1, 0),
    (14, 1, 1),
)


def kernel(
    tok, wg, wu, wd, grd,
    out_ref, tg_ref, dg_ref, du_ref, dd_ref,
    act, w, rs_send, rs_recv, hall, gu, q, ps, pr, sa, ra, sb, rb, sc, rc,
    dw, outs, local_sem, out_sem, sent, r1, r2, r3, rp, zr, ar, prs, ras, rbs, rcs,
):
    c = lax.axis_index("gx")
    gy = lax.axis_index("gy")
    z = lax.axis_index("gz")
    y, x = gy // 4, gy % 4
    f = x * (1 - c) + y * c
    s = y * (1 - c) + x * c
    fm, sm = 1 + 3 * c, 4 - 3 * c
    sg = 1 - 2 * c
    partner = (1 - c, gy, z)

    def gy_of(f_, s_):
        return ((f_ + 8) % 4) * fm + ((s_ + 8) % 4) * sm

    def at_fs(f_, s_):
        return (c, gy_of(f_, s_), z)

    def mod8(k):
        return (k + 16) % 8

    def at_z(k):
        return (c, gy, mod8(z + k))

    def rows_of(r, block):
        return pl.ds(pl.multiple_of(16 * STARTS[r] + block * SIZES[r], 16), SIZES[r])

    def zrows(r, block):
        return pl.ds(pl.multiple_of(16 * STARTS[r] + block * 2 * SIZES[r], 16), 2 * SIZES[r])

    def round_rows(r):
        return pl.ds(16 * STARTS[r], 16 * SIZES[r])

    def cut(r):
        return pl.ds(STARTS[r], SIZES[r])

    def zcut(r):
        return pl.ds(2 * STARTS[r], 2 * SIZES[r])

    def send(src, dst, family, rs, device):
        pltpu.make_async_remote_copy(
            src_ref=src, dst_ref=dst, send_sem=sent.at[family], recv_sem=rs,
            device_id=device, device_id_type=MESH,
        ).start()

    def recv(dst, rs):
        pltpu.make_async_remote_copy(
            src_ref=dst, dst_ref=dst, send_sem=sent.at[0], recv_sem=rs,
            device_id=partner, device_id_type=MESH,
        ).wait_recv()

    def all_sent(family, ref):
        pltpu.make_async_remote_copy(
            src_ref=ref, dst_ref=ref, send_sem=sent.at[family], recv_sem=local_sem.at[0],
            device_id=partner, device_id_type=MESH,
        ).wait_send()

    barrier = pltpu.get_barrier_semaphore()
    peers = [
        at_fs(f + 1, s), at_fs(f + 2, s), at_fs(f + 3, s), at_fs(f, s + 1), at_fs(f, s + 3),
        at_z(1), at_z(-1), partner,
    ]
    for peer in peers:
        pl.semaphore_signal(barrier, inc=1, device_id=peer, device_id_type=MESH)

    own = (tok, grd)

    def own_rows(a, r):
        return own[a].at[cut(r)]

    locals_ = [
        pltpu.make_async_copy(ref, w.at[k], local_sem.at[k]) for k, ref in enumerate((wg, wu, wd))
    ] + [
        pltpu.make_async_copy(
            own_rows(a, r), act.at[a, c, rows_of(r, gy)], local_sem.at[3 + 2 * r + a]
        )
        for r in range(ROUNDS) for a in range(2)
    ]
    for copy in locals_:
        copy.start()
    pl.semaphore_wait(barrier, len(peers))

    def act_block(a, r, k, t):
        return act.at[a, c, rows_of(r, gy_of(f - k, s + t))]

    def to_partner(a, r, k, t, src=None):
        ref = act_block(a, r, k, t)
        send(
            ref if src is None else src, ref,
            3, rp.at[a, r], partner,
        )

    def gather_own(a, r):
        src = own_rows(a, r)
        ref = act_block(a, r, 0, 0)
        for k in (1, 3, 2):
            send(src, ref, 0, r1.at[a, r, k], at_fs(f + k, s))
        send(src, ref, 1, r2.at[a, r, 0, 0], at_fs(f, s + 1))
        send(src, ref, 1, r2.at[a, r, 1, 0], at_fs(f, s + 3))
        to_partner(a, r, 0, 0, src)

    def gather_row(a, r, k):
        ref = act_block(a, r, k, 0)
        recv(ref, r1.at[a, r, k])
        send(ref, ref, 1, r2.at[a, r, 0, k], at_fs(f, s + 1))
        send(ref, ref, 1, r2.at[a, r, 1, k], at_fs(f, s + 3))
        to_partner(a, r, k, 0)

    def gather_near(a, r, way, k):
        t = (3, 1)[way]
        ref = act_block(a, r, k, t)
        recv(ref, r2.at[a, r, way, k])
        if (way == 0) == (k < 2):
            send(ref, ref, 2, r3.at[a, r, k], at_fs(f, s + 1 + 2 * way))
        to_partner(a, r, k, t)

    def gather_far(a, r, k):
        ref = act_block(a, r, k, 2)
        recv(ref, r3.at[a, r, k])
        to_partner(a, r, k, 2)

    def gather_end(a, r):
        recv(act.at[a, 1 - c, round_rows(r)], rp.at[a, r])
        locals_[3 + 2 * r + a].wait()

    def part(a, r, d):
        rows = zrows(r, d)
        source = 0 if a < 2 else 1
        return dot_plain(act[source, 0, rows, :], w[a, 0:512, :]) + dot_plain(
            act[source, 1, rows, :], w[a, 512:1024, :]
        )

    def sum_recv(a, r, slot):
        recv(rs_recv.at[a, slot, zcut(r)], zr.at[a, r, slot])
        return rs_recv[a, slot, zcut(r), :].astype(F32)

    def sum_step(a, r, j, way):
        slot = 4 * way + j
        to = (-sg, sg)[way]
        value = part(a, r, mod8(z + to * (4 - way - j)))
        if j > 0:
            value = value + sum_recv(a, r, slot - 1)
        rs_send[a, slot, zcut(r), :] = value.astype(BF16)
        send(
            rs_send.at[a, slot, zcut(r)], rs_recv.at[a, slot, zcut(r)],
            4, zr.at[a, r, slot], at_z(to),
        )

    def sum_end(a, r):
        value = part(a, r, z)
        for slot in (3, 6):
            value = value + sum_recv(a, r, slot)
        return value

    def zgather(t, r, j, way):
        slot = 4 * way + j
        to = (-sg, sg)[way]
        ref = hall.at[t, zrows(r, mod8(z - to * j))]
        if j > 0:
            recv(ref, ar.at[t, r, slot - 1])
        if j < 4 - way:
            send(ref, ref, 5, ar.at[t, r, slot], at_z(to))

    def product(o, r, b, half):
        rows = zrows(r, b)
        cols = pl.ds(pl.multiple_of(half * 512, 512), 512)
        if o == 0:
            return dot_last(hall[0, rows, :], w[2, cols, :])
        return dot_last(hall[1, rows, :], w[0, cols, :]) + dot_last(hall[2, rows, :], w[1, cols, :])

    def out_block(o, r, j, way):
        b = mod8(z + (sg, -sg)[way] * j)
        rows = zrows(r, b)
        ps[o, rows, :] = product(o, r, b, 1 - c).astype(BF16)
        send(ps.at[o, rows], pr.at[o, rows], 6, prs.at[o, r], partner)
        q[o, rows, :] = product(o, r, b, c)

    def out_pair(o, r):
        recv(pr.at[o, round_rows(r)], prs.at[o, r])

    done = []

    def put(k, src, dst):
        copy = pltpu.make_async_copy(src, dst, out_sem.at[k])
        copy.start()
        done.append(copy)

    def chip_sum(o, r, k, t):
        rows = rows_of(r, gy_of(f + k, s + t))
        return q[o, rows, :] + pr[o, rows, :].astype(F32)

    def stage_a(o, r, k):
        sa[o, k, cut(r), :] = chip_sum(o, r, k, 2).astype(BF16)
        send(
            sa.at[o, k, cut(r)], ra.at[o, k, cut(r)], 7, ras.at[o, r, k],
            at_fs(f, s + (1 if k < 2 else 3)),
        )

    def stage_b(o, r, way, k):
        t = (1, 3)[way]
        slot = 4 * way + k
        value = chip_sum(o, r, k, t)
        if (way == 0) == (k < 2):
            recv(ra.at[o, k, cut(r)], ras.at[o, r, k])
            value = value + ra[o, k, cut(r), :].astype(F32)
        sb[o, slot, cut(r), :] = value.astype(BF16)
        send(
            sb.at[o, slot, cut(r)], rb.at[o, slot, cut(r)],
            8, rbs.at[o, r, slot], at_fs(f, s + t),
        )

    def stage_c(o, r, k):
        value = chip_sum(o, r, k, 0)
        for slot in (k, 4 + k):
            recv(rb.at[o, slot, cut(r)], rbs.at[o, r, slot])
            value = value + rb[o, slot, cut(r), :].astype(F32)
        if k > 0:
            sc[o, k, cut(r), :] = value.astype(BF16)
            send(
                sc.at[o, k, cut(r)], rc.at[o, k, cut(r)], 9, rcs.at[o, r, k],
                at_fs(f + k, s),
            )
        else:
            q[o, rows_of(r, gy), :] = value

    def stage_d(o, r):
        value = q[o, rows_of(r, gy), :]
        for k in (1, 3, 2):
            recv(rc.at[o, k, cut(r)], rcs.at[o, r, k])
            value = value + rc[o, k, cut(r), :].astype(F32)
        outs[o, cut(r), :] = value.astype(BF16)
        if r == ROUNDS - 1:
            put(o, outs.at[o], (out_ref, tg_ref)[o])

    def weight_grad(k):
        ref, a, t = ((dg_ref, 0, 1), (du_ref, 0, 2), (dd_ref, 1, 0))[k]
        for half in range(2):
            dw[k, half * 512:(half + 1) * 512, :] = dot_first(act[a, half], hall[t])
        put(2 + k, dw.at[k], ref)

    def forward(r):
        gate = sum_end(0, r)
        gu[0, zcut(r), :] = gate
        gated = gate * jax.nn.sigmoid(gate)
        up = sum_end(1, r)
        gu[1, zcut(r), :] = up
        hall[0, zrows(r, z), :] = (gated * up).astype(BF16)
        for way in range(2):
            zgather(0, r, 0, way)

    def backward(r):
        hidden_grad = sum_end(2, r)
        gate = gu[0, zcut(r), :]
        up = gu[1, zcut(r), :]
        sigmoid = jax.nn.sigmoid(gate)
        hall[1, zrows(r, z), :] = (
            hidden_grad * up * sigmoid * (1.0 + gate * (1.0 - sigmoid))
        ).astype(BF16)
        hall[2, zrows(r, z), :] = (hidden_grad * (gate * sigmoid)).astype(BF16)
        for t in (1, 2):
            for way in range(2):
                zgather(t, r, 0, way)

    def weights():
        for copy in locals_[:3]:
            copy.wait()

    phases = (
        gather_own, gather_row, gather_near, gather_far, gather_end, sum_step, forward, backward,
        zgather, out_block, out_pair, stage_a, stage_b, stage_c, stage_d, weight_grad, weights,
    )
    for kind, *rest in ORDER:
        phases[kind](*rest)
    for family, ref in enumerate((
        act.at[0, 0, pl.ds(0, 768)], act.at[0, 0], act.at[0, 0, pl.ds(0, 1024)], act.at[:, 0],
        rs_send, rs_send, ps, sa, sb, sc.at[:, pl.ds(1, 3)],
    )):
        all_sent(family, ref)
    for copy in done:
        copy.wait()


def put_out(*refs):
    sems = refs[10]
    copies = [pltpu.make_async_copy(refs[k], refs[5 + k], sems.at[k]) for k in range(5)]
    for copy in copies:
        copy.start()
    for copy in copies:
        copy.wait()


def per_device(tokens, gate_weight, up_weight, down_weight, out_grad):
    dma = pltpu.SemaphoreType.DMA
    vmem = pltpu.VMEM

    results = pl.pallas_call(
        kernel,
        out_shape=(
            pltpu.VMEM((128, 512), BF16),
            pltpu.VMEM((128, 512), BF16),
            pltpu.VMEM((1024, 256), F32),
            pltpu.VMEM((1024, 256), F32),
            pltpu.VMEM((1024, 256), F32),
        ),
        in_specs=[pl.BlockSpec(memory_space=pltpu.HBM)] * 5,
        out_specs=tuple([pl.BlockSpec(memory_space=pl.ANY)] * 5),
        scratch_shapes=[
            vmem((2, 2, 2048, 512), BF16),
            vmem((3, 1024, 256), BF16),
            vmem((3, 7, 256, 256), BF16),
            vmem((3, 7, 256, 256), BF16),
            vmem((3, 2048, 256), BF16),
            vmem((2, 256, 256), F32),
            vmem((2, 2048, 512), F32),
            vmem((2, 2048, 512), BF16),
            vmem((2, 2048, 512), BF16),
            vmem((2, 4, 128, 512), BF16),
            vmem((2, 4, 128, 512), BF16),
            vmem((2, 8, 128, 512), BF16),
            vmem((2, 8, 128, 512), BF16),
            vmem((2, 4, 128, 512), BF16),
            vmem((2, 4, 128, 512), BF16),
            vmem((3, 1024, 256), F32),
            vmem((2, 128, 512), BF16),
            dma((3 + 2 * ROUNDS,)),
            dma((5,)),
            dma((10,)),
            dma((2, ROUNDS, 4)),
            dma((2, ROUNDS, 2, 4)),
            dma((2, ROUNDS, 4)),
            dma((2, ROUNDS)),
            dma((3, ROUNDS, 7)),
            dma((3, ROUNDS, 7)),
            dma((2, ROUNDS)),
            dma((2, ROUNDS, 4)),
            dma((2, ROUNDS, 8)),
            dma((2, ROUNDS, 4)),
        ],
        compiler_params=pltpu.CompilerParams(
            collective_id=0, has_side_effects=True, vmem_limit_bytes=56 * 1024 * 1024
        ),
        name="slab",
    )(tokens, gate_weight, up_weight, down_weight, out_grad)

    shapes = tuple(jax.ShapeDtypeStruct(value.shape, value.dtype) for value in results)
    return pl.pallas_call(
        put_out,
        out_shape=shapes,
        in_specs=[pl.BlockSpec(memory_space=pl.ANY)] * 5,
        out_specs=tuple([pl.BlockSpec(memory_space=pltpu.HBM)] * 5),
        scratch_shapes=[dma((5,))],
        compiler_params=pltpu.CompilerParams(vmem_limit_bytes=1024 * 1024),
        name="put_out",
    )(*results)


def solution(mesh):
    return jax.shard_map(
        per_device,
        mesh=mesh,
        in_specs=(
            P("gy", ("gz", "gx")),
            P("gz", ("gx", "gy")),
            P("gz", ("gx", "gy")),
            P("gz", ("gx", "gy")),
            P("gy", ("gz", "gx")),
        ),
        out_specs=(
            P("gy", ("gz", "gx")),
            P("gy", ("gz", "gx")),
            P("gz", ("gx", "gy")),
            P("gz", ("gx", "gy")),
            P("gz", ("gx", "gy")),
        ),
        check_vma=False,
    )
```

```python
import jax
import jax.numpy as jnp
from jax import lax
from jax.experimental import pallas as pl
from jax.experimental.pallas import tpu as pltpu
from jax.sharding import PartitionSpec as P

MESH = pl.DeviceIdType.MESH
F32 = jnp.float32
BF16 = jnp.bfloat16


def dot_plain(left, right):
    return jnp.dot(left, right, preferred_element_type=F32)


def dot_last(left, right):
    return lax.dot_general(left, right, (((1,), (1,)), ((), ())), preferred_element_type=F32)


def dot_first(left, right):
    return lax.dot_general(left, right, (((0,), (0,)), ((), ())), preferred_element_type=F32)


SIZES = (48, 32, 48,)
STARTS = tuple(sum(SIZES[:r]) for r in range(len(SIZES)))
ROUNDS = len(SIZES)

ORDER = (
    (0, 0, 0), (16,), (2, 0, 0, 1, 0), (1, 0, 0, 3), (1, 0, 0, 1), (2, 0, 0, 0, 0), (1, 0, 0, 2), (0, 0, 1),
    (2, 0, 0, 1, 3), (2, 0, 0, 0, 3), (2, 0, 0, 1, 1), (2, 0, 0, 0, 1), (3, 0, 0, 0), (1, 0, 1, 3),
    (2, 0, 0, 1, 2), (1, 0, 1, 1), (2, 0, 0, 0, 2), (2, 0, 1, 1, 0), (2, 0, 1, 0, 0), (3, 0, 0, 3),
    (1, 0, 1, 2), (0, 0, 2), (3, 0, 0, 1), (2, 0, 1, 1, 3), (2, 0, 1, 0, 3), (2, 0, 1, 0, 1), (3, 0, 0, 2),
    (3, 0, 1, 0), (2, 0, 1, 1, 1), (4, 0, 0), (5, 0, 0, 0, 0), (5, 1, 0, 0, 0), (2, 0, 1, 1, 2),
    (5, 0, 0, 0, 1), (2, 0, 1, 0, 2), (5, 1, 0, 0, 1), (1, 0, 2, 3), (2, 0, 2, 1, 0), (1, 0, 2, 1),
    (3, 0, 1, 3), (2, 0, 2, 0, 0), (3, 0, 1, 1), (1, 0, 2, 2), (0, 1, 0), (5, 0, 0, 1, 0), (3, 0, 1, 2),
    (5, 1, 0, 1, 0), (5, 0, 0, 1, 1), (2, 0, 2, 0, 3), (5, 1, 0, 1, 1), (2, 0, 2, 1, 3), (4, 0, 1),
    (5, 0, 1, 0, 1), (2, 0, 2, 0, 1), (2, 0, 2, 1, 1), (5, 1, 1, 0, 0), (5, 0, 1, 0, 0), (5, 1, 1, 0, 1),
    (3, 0, 2, 0), (5, 0, 0, 2, 0), (2, 0, 2, 1, 2), (1, 1, 0, 3), (5, 1, 0, 2, 0), (1, 1, 0, 1),
    (2, 1, 0, 1, 0), (2, 0, 2, 0, 2), (5, 0, 0, 2, 1), (2, 1, 0, 0, 0), (3, 0, 2, 3), (5, 1, 0, 2, 1),
    (5, 1, 1, 1, 0), (5, 0, 1, 1, 1), (3, 0, 2, 1), (1, 1, 0, 2), (0, 1, 1), (5, 0, 1, 1, 0), (5, 1, 1, 1, 1),
    (3, 0, 2, 2), (5, 0, 0, 3, 0), (2, 1, 0, 0, 3), (2, 1, 0, 1, 3), (2, 1, 0, 0, 1), (5, 1, 0, 3, 0),
    (4, 0, 2), (2, 1, 0, 1, 1), (5, 0, 2, 0, 1), (3, 1, 0, 0), (5, 0, 2, 0, 0), (5, 1, 1, 2, 0),
    (5, 1, 2, 0, 0), (5, 1, 2, 0, 1), (5, 0, 1, 2, 0), (1, 1, 1, 3), (5, 0, 1, 2, 1), (2, 1, 0, 1, 2),
    (1, 1, 1, 1), (2, 1, 0, 0, 2), (2, 1, 1, 1, 0), (5, 1, 1, 2, 1), (2, 1, 1, 0, 0), (3, 1, 0, 3), (6, 0),
    (3, 1, 0, 1), (1, 1, 1, 2), (0, 1, 2), (9, 0, 0, 0, 0), (5, 0, 2, 1, 0), (5, 0, 2, 1, 1), (5, 1, 1, 3, 0),
    (2, 1, 1, 1, 3), (2, 1, 1, 0, 3), (5, 1, 2, 1, 1), (2, 1, 1, 0, 1), (3, 1, 0, 2), (3, 1, 1, 0),
    (5, 1, 2, 1, 0), (2, 1, 1, 1, 1), (5, 0, 1, 3, 0), (4, 1, 0), (5, 2, 0, 0, 1), (5, 2, 0, 0, 0),
    (8, 0, 0, 1, 1), (9, 0, 0, 1, 1), (2, 1, 1, 1, 2), (2, 1, 1, 0, 2), (8, 0, 0, 1, 0), (9, 0, 0, 1, 0),
    (1, 1, 2, 3), (2, 1, 2, 1, 0), (5, 0, 2, 2, 1), (1, 1, 2, 1), (3, 1, 1, 3), (5, 0, 2, 2, 0),
    (2, 1, 2, 0, 0), (3, 1, 1, 1), (5, 1, 2, 2, 1), (1, 1, 2, 2), (5, 1, 2, 2, 0), (5, 2, 0, 1, 1), (6, 1),
    (3, 1, 1, 2), (8, 0, 0, 2, 1), (9, 0, 0, 2, 1), (2, 1, 2, 0, 3), (2, 1, 2, 1, 3), (5, 2, 0, 1, 0),
    (9, 0, 1, 0, 0), (2, 1, 2, 0, 1), (2, 1, 2, 1, 1), (4, 1, 1), (3, 1, 2, 0), (5, 2, 1, 0, 1),
    (2, 1, 2, 1, 2), (8, 0, 0, 2, 0), (9, 0, 0, 2, 0), (2, 1, 2, 0, 2), (5, 2, 1, 0, 0), (5, 0, 2, 3, 0),
    (5, 2, 0, 2, 1), (5, 1, 2, 3, 0), (8, 0, 1, 1, 1), (9, 0, 1, 1, 1), (3, 1, 2, 3), (8, 0, 1, 1, 0),
    (9, 0, 1, 1, 0), (3, 1, 2, 1), (8, 0, 0, 3, 1), (9, 0, 0, 3, 1), (3, 1, 2, 2), (5, 2, 0, 2, 0),
    (5, 2, 1, 1, 1), (8, 0, 0, 3, 0), (9, 0, 0, 3, 0), (4, 1, 2), (5, 2, 2, 0, 0), (5, 2, 1, 1, 0),
    (5, 2, 2, 0, 1), (8, 0, 1, 2, 1), (9, 0, 1, 2, 1), (6, 2), (5, 2, 1, 2, 1), (8, 0, 1, 2, 0),
    (9, 0, 1, 2, 0), (5, 2, 0, 3, 0), (8, 0, 0, 4, 0), (9, 0, 0, 4, 0), (9, 0, 2, 0, 0), (5, 2, 2, 1, 1),
    (5, 2, 2, 1, 0), (8, 0, 1, 3, 1), (9, 0, 1, 3, 1), (10, 0, 0), (11, 0, 0, 0), (11, 0, 0, 2), (11, 0, 0, 1),
    (11, 0, 0, 3), (12, 0, 0, 1, 1), (12, 0, 0, 1, 0), (12, 0, 0, 0, 2), (5, 2, 1, 2, 0), (12, 0, 0, 0, 3),
    (8, 0, 2, 1, 1), (8, 0, 2, 1, 0), (9, 0, 2, 1, 1), (9, 0, 2, 1, 0), (8, 0, 1, 3, 0), (9, 0, 1, 3, 0),
    (7, 0), (9, 1, 0, 0, 0), (12, 0, 0, 0, 0), (12, 0, 0, 1, 2), (5, 2, 2, 2, 0), (5, 2, 1, 3, 0),
    (12, 0, 0, 0, 1), (12, 0, 0, 1, 3), (5, 2, 2, 2, 1), (8, 0, 2, 2, 1), (8, 0, 2, 2, 0), (9, 0, 2, 2, 1),
    (8, 0, 1, 4, 0), (9, 0, 1, 4, 0), (9, 0, 2, 2, 0), (8, 1, 0, 1, 0), (8, 1, 0, 1, 1), (10, 0, 1),
    (11, 0, 1, 3), (11, 0, 1, 0), (11, 0, 1, 2), (11, 0, 1, 1), (12, 0, 1, 1, 0), (13, 0, 0, 0), (13, 0, 0, 2),
    (12, 0, 1, 0, 3), (12, 0, 1, 0, 2), (8, 2, 0, 1, 0), (8, 2, 0, 1, 1), (9, 1, 0, 1, 0), (13, 0, 0, 1),
    (9, 1, 0, 1, 1), (13, 0, 0, 3), (5, 2, 2, 3, 0), (7, 1), (9, 1, 1, 0, 0), (12, 0, 1, 0, 0),
    (12, 0, 1, 1, 3), (12, 0, 1, 1, 1), (12, 0, 1, 1, 2), (8, 0, 2, 3, 1), (8, 1, 0, 2, 1), (9, 0, 2, 3, 1),
    (12, 0, 1, 0, 1), (8, 0, 2, 3, 0), (9, 0, 2, 3, 0), (8, 1, 0, 2, 0), (8, 2, 0, 2, 1), (9, 1, 0, 2, 1),
    (8, 2, 0, 2, 0), (9, 1, 0, 2, 0), (8, 1, 1, 1, 1), (7, 2), (14, 0, 0), (8, 2, 1, 1, 1), (8, 1, 1, 1, 0),
    (13, 0, 1, 3), (9, 1, 1, 1, 1), (13, 0, 1, 0), (8, 2, 1, 1, 0), (13, 0, 1, 1), (13, 0, 1, 2),
    (8, 1, 0, 3, 1), (9, 1, 1, 1, 0), (9, 1, 2, 0, 0), (8, 2, 0, 3, 1), (9, 1, 0, 3, 1), (8, 0, 2, 4, 0),
    (8, 1, 1, 2, 1), (9, 0, 2, 4, 0), (8, 1, 0, 3, 0), (15, 2), (8, 2, 0, 3, 0), (9, 1, 0, 3, 0),
    (8, 1, 2, 1, 0), (8, 1, 2, 1, 1), (10, 0, 2), (11, 0, 2, 2), (11, 0, 2, 1), (11, 0, 2, 3), (8, 2, 1, 2, 1),
    (9, 1, 1, 2, 1), (14, 0, 1), (8, 1, 1, 3, 1), (11, 0, 2, 0), (12, 0, 2, 1, 0), (12, 0, 2, 0, 3),
    (8, 1, 1, 2, 0), (12, 0, 2, 0, 2), (8, 2, 2, 1, 0), (9, 1, 2, 1, 0), (8, 2, 1, 2, 0), (9, 1, 1, 2, 0),
    (8, 1, 0, 4, 0), (12, 0, 2, 1, 1), (8, 2, 2, 1, 1), (9, 1, 2, 1, 1), (8, 2, 0, 4, 0), (9, 1, 0, 4, 0),
    (8, 1, 2, 2, 1), (12, 0, 2, 0, 1), (12, 0, 2, 1, 2), (8, 1, 2, 2, 0), (8, 2, 1, 3, 1), (9, 1, 1, 3, 1),
    (8, 1, 1, 3, 0), (12, 0, 2, 1, 3), (12, 0, 2, 0, 0), (8, 2, 2, 2, 0), (9, 1, 2, 2, 0), (10, 1, 0),
    (11, 1, 0, 1), (11, 1, 0, 3), (11, 1, 0, 0), (11, 1, 0, 2), (12, 1, 0, 1, 0), (12, 1, 0, 0, 2),
    (12, 1, 0, 0, 3), (12, 1, 0, 1, 1), (8, 2, 1, 3, 0), (9, 1, 1, 3, 0), (8, 2, 2, 2, 1), (9, 1, 2, 2, 1),
    (8, 1, 2, 3, 1), (8, 1, 2, 3, 0), (13, 0, 2, 2), (13, 0, 2, 1), (8, 1, 1, 4, 0), (8, 2, 2, 3, 0),
    (9, 1, 2, 3, 0), (13, 0, 2, 3), (13, 0, 2, 0), (8, 2, 1, 4, 0), (9, 1, 1, 4, 0), (12, 1, 0, 1, 3),
    (12, 1, 0, 0, 1), (12, 1, 0, 0, 0), (12, 1, 0, 1, 2), (8, 2, 2, 3, 1), (9, 1, 2, 3, 1), (8, 1, 2, 4, 0),
    (10, 1, 1), (11, 1, 1, 3), (11, 1, 1, 0), (11, 1, 1, 2), (11, 1, 1, 1), (12, 1, 1, 1, 0), (12, 1, 1, 1, 1),
    (12, 1, 1, 0, 2), (12, 1, 1, 0, 3), (8, 2, 2, 4, 0), (9, 1, 2, 4, 0), (13, 1, 0, 3), (10, 1, 2),
    (11, 1, 2, 2), (11, 1, 2, 0), (11, 1, 2, 1), (11, 1, 2, 3), (13, 1, 0, 1), (13, 1, 0, 2), (12, 1, 2, 0, 2),
    (12, 1, 2, 1, 0), (12, 1, 2, 1, 1), (12, 1, 2, 0, 3), (12, 1, 1, 1, 3), (14, 0, 2), (13, 1, 0, 0),
    (12, 1, 1, 1, 2), (12, 1, 1, 0, 0), (12, 1, 1, 0, 1), (12, 1, 2, 1, 2), (12, 1, 2, 0, 0), (15, 1),
    (12, 1, 2, 0, 1), (12, 1, 2, 1, 3), (15, 0), (13, 1, 1, 2), (13, 1, 1, 3), (14, 1, 0), (13, 1, 2, 2),
    (13, 1, 1, 0), (13, 1, 1, 1), (13, 1, 2, 0), (13, 1, 2, 1), (13, 1, 2, 3), (14, 1, 1), (14, 1, 2),
)


def kernel(
    tok, wg, wu, wd, grd,
    out_ref, tg_ref, dg_ref, du_ref, dd_ref,
    act, w, rs_send, rs_recv, hall, gu, q, ps, pr, sa, ra, sb, rb, sc, rc,
    dw, outs, local_sem, out_sem, sent, r1, r2, r3, rp, zr, ar, prs, ras, rbs, rcs,
):
    c = lax.axis_index("gx")
    gy = lax.axis_index("gy")
    z = lax.axis_index("gz")
    y, x = gy // 4, gy % 4
    f = x * (1 - c) + y * c
    s = y * (1 - c) + x * c
    fm, sm = 1 + 3 * c, 4 - 3 * c
    sg = 1 - 2 * c
    partner = (1 - c, gy, z)

    def gy_of(f_, s_):
        return ((f_ + 8) % 4) * fm + ((s_ + 8) % 4) * sm

    def at_fs(f_, s_):
        return (c, gy_of(f_, s_), z)

    def mod8(k):
        return (k + 16) % 8

    def at_z(k):
        return (c, gy, mod8(z + k))

    def rows_of(r, block):
        return pl.ds(pl.multiple_of(16 * STARTS[r] + block * SIZES[r], 16), SIZES[r])

    def zrows(r, block):
        return pl.ds(pl.multiple_of(16 * STARTS[r] + block * 2 * SIZES[r], 16), 2 * SIZES[r])

    def round_rows(r):
        return pl.ds(16 * STARTS[r], 16 * SIZES[r])

    def cut(r):
        return pl.ds(STARTS[r], SIZES[r])

    def zcut(r):
        return pl.ds(2 * STARTS[r], 2 * SIZES[r])

    def send(src, dst, family, rs, device):
        pltpu.make_async_remote_copy(
            src_ref=src, dst_ref=dst, send_sem=sent.at[family], recv_sem=rs,
            device_id=device, device_id_type=MESH,
        ).start()

    def recv(dst, rs):
        pltpu.make_async_remote_copy(
            src_ref=dst, dst_ref=dst, send_sem=sent.at[0], recv_sem=rs,
            device_id=partner, device_id_type=MESH,
        ).wait_recv()

    def all_sent(family, ref):
        pltpu.make_async_remote_copy(
            src_ref=ref, dst_ref=ref, send_sem=sent.at[family], recv_sem=local_sem.at[0],
            device_id=partner, device_id_type=MESH,
        ).wait_send()

    barrier = pltpu.get_barrier_semaphore()
    peers = [
        at_fs(f + 1, s), at_fs(f + 2, s), at_fs(f + 3, s), at_fs(f, s + 1), at_fs(f, s + 3),
        at_z(1), at_z(-1), partner,
    ]
    for peer in peers:
        pl.semaphore_signal(barrier, inc=1, device_id=peer, device_id_type=MESH)

    own = (tok, grd)

    def own_rows(a, r):
        return own[a].at[cut(r)]

    locals_ = [
        pltpu.make_async_copy(ref, w.at[k], local_sem.at[k]) for k, ref in enumerate((wg, wu, wd))
    ] + [
        pltpu.make_async_copy(
            own_rows(a, r), act.at[a, c, rows_of(r, gy)], local_sem.at[3 + 2 * r + a]
        )
        for r in range(ROUNDS) for a in range(2)
    ]
    for copy in locals_[3:] + locals_[:3]:
        copy.start()
    pl.semaphore_wait(barrier, len(peers))

    def act_block(a, r, k, t):
        return act.at[a, c, rows_of(r, gy_of(f - k, s + t))]

    def to_partner(a, r, k, t, src=None):
        ref = act_block(a, r, k, t)
        send(
            ref if src is None else src, ref,
            3, rp.at[a, r], partner,
        )

    def gather_own(a, r):
        ref = src = act_block(a, r, 0, 0)
        locals_[3 + 2 * r + a].wait()
        for k in (1, 3, 2):
            send(src, ref, 0, r1.at[a, r, k - 1], at_fs(f + k, s))
        send(src, ref, 1, r2.at[a, r, 0, 0], at_fs(f, s + 1))
        send(src, ref, 1, r2.at[a, r, 1, 0], at_fs(f, s + 3))
        to_partner(a, r, 0, 0, src)

    def gather_row(a, r, k):
        ref = act_block(a, r, k, 0)
        recv(ref, r1.at[a, r, k - 1])
        send(ref, ref, 1, r2.at[a, r, 0, k], at_fs(f, s + 1))
        send(ref, ref, 1, r2.at[a, r, 1, k], at_fs(f, s + 3))
        to_partner(a, r, k, 0)

    def gather_near(a, r, way, k):
        t = (3, 1)[way]
        ref = act_block(a, r, k, t)
        recv(ref, r2.at[a, r, way, k])
        if (way == 0) == (k < 2):
            send(ref, ref, 2, r3.at[a, r, k], at_fs(f, s + 1 + 2 * way))
        to_partner(a, r, k, t)

    def gather_far(a, r, k):
        ref = act_block(a, r, k, 2)
        recv(ref, r3.at[a, r, k])
        to_partner(a, r, k, 2)

    def gather_end(a, r):
        recv(act.at[a, 1 - c, round_rows(r)], rp.at[a, r])

    def part(a, r, d):
        rows = zrows(r, d)
        source = 0 if a < 2 else 1
        return dot_plain(act[source, 0, rows, :], w[a, 0:512, :]) + dot_plain(
            act[source, 1, rows, :], w[a, 512:1024, :]
        )

    def sum_recv(a, r, slot):
        recv(rs_recv.at[a, slot, zcut(r)], zr.at[a, r, slot])
        return rs_recv[a, slot, zcut(r), :].astype(F32)

    def sum_step(a, r, j, way):
        slot = 4 * way + j
        to = (-sg, sg)[way]
        value = part(a, r, mod8(z + to * (4 - way - j)))
        if j > 0:
            value = value + sum_recv(a, r, slot - 1)
        rs_send[a, slot, zcut(r), :] = value.astype(BF16)
        send(
            rs_send.at[a, slot, zcut(r)], rs_recv.at[a, slot, zcut(r)],
            4, zr.at[a, r, slot], at_z(to),
        )

    def sum_end(a, r):
        value = part(a, r, z)
        for slot in (3, 6):
            value = value + sum_recv(a, r, slot)
        return value

    def zgather(t, r, j, way):
        slot = 4 * way + j
        to = (-sg, sg)[way]
        ref = hall.at[t, zrows(r, mod8(z - to * j))]
        if j > 0:
            recv(ref, ar.at[t, r, slot - 1])
        if j < 4 - way:
            send(ref, ref, 5, ar.at[t, r, slot], at_z(to))

    def product(o, r, b, half):
        rows = zrows(r, b)
        cols = pl.ds(pl.multiple_of(half * 512, 512), 512)
        if o == 0:
            return dot_last(hall[0, rows, :], w[2, cols, :])
        return dot_last(hall[1, rows, :], w[0, cols, :]) + dot_last(hall[2, rows, :], w[1, cols, :])

    def out_block(o, r, j, way):
        b = mod8(z + (sg, -sg)[way] * j)
        rows = zrows(r, b)
        ps[o, rows, :] = product(o, r, b, 1 - c).astype(BF16)
        send(ps.at[o, rows], pr.at[o, rows], 6, prs.at[o, r], partner)
        q[o, rows, :] = product(o, r, b, c)

    def out_pair(o, r):
        recv(pr.at[o, round_rows(r)], prs.at[o, r])

    done = []

    def put(k, src, dst):
        copy = pltpu.make_async_copy(src, dst, out_sem.at[k])
        copy.start()
        done.append(copy)

    def chip_sum(o, r, k, t):
        rows = rows_of(r, gy_of(f + k, s + t))
        return q[o, rows, :] + pr[o, rows, :].astype(F32)

    def stage_a(o, r, k):
        sa[o, k, cut(r), :] = chip_sum(o, r, k, 2).astype(BF16)
        send(
            sa.at[o, k, cut(r)], ra.at[o, k, cut(r)], 7, ras.at[o, r, k],
            at_fs(f, s + (1 if k < 2 else 3)),
        )

    def stage_b(o, r, way, k):
        t = (1, 3)[way]
        value = chip_sum(o, r, k, t)
        if (way == 0) == (k < 2):
            recv(ra.at[o, k, cut(r)], ras.at[o, r, k])
            value = value + ra[o, k, cut(r), :].astype(F32)
        sb[o, k, way, cut(r), :] = value.astype(BF16)
        send(
            sb.at[o, k, way, cut(r)], rb.at[o, k, way, cut(r)],
            8, rbs.at[o, r, k], at_fs(f, s + t),
        )

    def stage_c(o, r, k):
        value = chip_sum(o, r, k, 0)
        recv(rb.at[o, k, :, cut(r)], rbs.at[o, r, k])
        for way in range(2):
            value = value + rb[o, k, way, cut(r), :].astype(F32)
        if k > 0:
            sc[o, k, cut(r), :] = value.astype(BF16)
            send(
                sc.at[o, k, cut(r)], rc.at[o, k, cut(r)], 9, rcs.at[o, r],
                at_fs(f + k, s),
            )
        else:
            q[o, rows_of(r, gy), :] = value

    def stage_d(o, r):
        value = q[o, rows_of(r, gy), :]
        recv(rc.at[o, pl.ds(1, 3), cut(r)], rcs.at[o, r])
        for k in (1, 3, 2):
            value = value + rc[o, k, cut(r), :].astype(F32)
        outs[o, cut(r), :] = value.astype(BF16)
        if r == ROUNDS - 1:
            put(o, outs.at[o], (out_ref, tg_ref)[o])

    def weight_grad(k):
        ref, a, t = ((dg_ref, 0, 1), (du_ref, 0, 2), (dd_ref, 1, 0))[k]
        for half in range(2):
            dw[k, half * 512:(half + 1) * 512, :] = dot_first(act[a, half], hall[t])
        put(2 + k, dw.at[k], ref)

    def forward(r):
        gate = sum_end(0, r)
        gu[0, zcut(r), :] = gate
        gated = gate * jax.nn.sigmoid(gate)
        up = sum_end(1, r)
        gu[1, zcut(r), :] = up
        hall[0, zrows(r, z), :] = (gated * up).astype(BF16)
        for way in range(2):
            zgather(0, r, 0, way)

    def backward(r):
        hidden_grad = sum_end(2, r)
        gate = gu[0, zcut(r), :]
        up = gu[1, zcut(r), :]
        sigmoid = jax.nn.sigmoid(gate)
        hall[1, zrows(r, z), :] = (
            hidden_grad * up * sigmoid * (1.0 + gate * (1.0 - sigmoid))
        ).astype(BF16)
        hall[2, zrows(r, z), :] = (hidden_grad * (gate * sigmoid)).astype(BF16)
        for t in (1, 2):
            for way in range(2):
                zgather(t, r, 0, way)

    def weights():
        for copy in locals_[:3]:
            copy.wait()

    phases = (
        gather_own, gather_row, gather_near, gather_far, gather_end, sum_step, forward, backward,
        zgather, out_block, out_pair, stage_a, stage_b, stage_c, stage_d, weight_grad, weights,
    )
    for kind, *rest in ORDER:
        phases[kind](*rest)
    for family, ref in enumerate((
        act.at[0, 0, pl.ds(0, 768)], act.at[0, 0], act.at[0, 0, pl.ds(0, 1024)], act.at[:, 0],
        rs_send, rs_send, ps, sa, sb, sc.at[:, pl.ds(1, 3)],
    )):
        all_sent(family, ref)
    for copy in done:
        copy.wait()


def put_out(*refs):
    sems = refs[10]
    copies = [pltpu.make_async_copy(refs[k], refs[5 + k], sems.at[k]) for k in range(2)] + [
        pltpu.make_async_copy(
            refs[k].at[pl.ds(256 * n, 256)], refs[5 + k].at[pl.ds(256 * n, 256)],
            sems.at[2 + 4 * (k - 2) + n],
        )
        for k in range(2, 5) for n in range(4)
    ]
    for copy in copies:
        copy.start()
    for copy in copies:
        copy.wait()


def per_device(tokens, gate_weight, up_weight, down_weight, out_grad):
    dma = pltpu.SemaphoreType.DMA
    vmem = pltpu.VMEM

    results = pl.pallas_call(
        kernel,
        out_shape=(
            pltpu.VMEM((128, 512), BF16),
            pltpu.VMEM((128, 512), BF16),
            pltpu.VMEM((1024, 256), F32),
            pltpu.VMEM((1024, 256), F32),
            pltpu.VMEM((1024, 256), F32),
        ),
        in_specs=[pl.BlockSpec(memory_space=pltpu.HBM)] * 5,
        out_specs=tuple([pl.BlockSpec(memory_space=pl.ANY)] * 5),
        scratch_shapes=[
            vmem((2, 2, 2048, 512), BF16),
            vmem((3, 1024, 256), BF16),
            vmem((3, 7, 256, 256), BF16),
            vmem((3, 7, 256, 256), BF16),
            vmem((3, 2048, 256), BF16),
            vmem((2, 256, 256), F32),
            vmem((2, 2048, 512), F32),
            vmem((2, 2048, 512), BF16),
            vmem((2, 2048, 512), BF16),
            vmem((2, 4, 128, 512), BF16),
            vmem((2, 4, 128, 512), BF16),
            vmem((2, 4, 2, 128, 512), BF16),
            vmem((2, 4, 2, 128, 512), BF16),
            vmem((2, 4, 128, 512), BF16),
            vmem((2, 4, 128, 512), BF16),
            vmem((3, 1024, 256), F32),
            vmem((2, 128, 512), BF16),
            dma((3 + 2 * ROUNDS,)),
            dma((5,)),
            dma((10,)),
            dma((2, ROUNDS, 3)),
            dma((2, ROUNDS, 2, 4)),
            dma((2, ROUNDS, 4)),
            dma((2, ROUNDS)),
            dma((3, ROUNDS, 7)),
            dma((3, ROUNDS, 7)),
            dma((2, ROUNDS)),
            dma((2, ROUNDS, 4)),
            dma((2, ROUNDS, 4)),
            dma((2, ROUNDS)),
        ],
        compiler_params=pltpu.CompilerParams(
            collective_id=0, has_side_effects=True, vmem_limit_bytes=56 * 1024 * 1024
        ),
        name="slab",
    )(tokens, gate_weight, up_weight, down_weight, out_grad)

    shapes = tuple(jax.ShapeDtypeStruct(value.shape, value.dtype) for value in results)
    return pl.pallas_call(
        put_out,
        out_shape=shapes,
        in_specs=[pl.BlockSpec(memory_space=pl.ANY)] * 5,
        out_specs=tuple([pl.BlockSpec(memory_space=pltpu.HBM)] * 5),
        scratch_shapes=[dma((14,))],
        compiler_params=pltpu.CompilerParams(vmem_limit_bytes=1024 * 1024),
        name="put_out",
    )(*results)


def solution(mesh):
    return jax.shard_map(
        per_device,
        mesh=mesh,
        in_specs=(
            P("gy", ("gz", "gx")),
            P("gz", ("gx", "gy")),
            P("gz", ("gx", "gy")),
            P("gz", ("gx", "gy")),
            P("gy", ("gz", "gx")),
        ),
        out_specs=(
            P("gy", ("gz", "gx")),
            P("gy", ("gz", "gx")),
            P("gz", ("gx", "gy")),
            P("gz", ("gx", "gy")),
            P("gz", ("gx", "gy")),
        ),
        check_vma=False,
    )
```

```python
import jax
import jax.numpy as jnp
from jax import lax
from jax.experimental import pallas as pl
from jax.experimental.pallas import tpu as pltpu
from jax.sharding import PartitionSpec as P

MESH = pl.DeviceIdType.MESH
F32 = jnp.float32
BF16 = jnp.bfloat16


def dot_plain(left, right):
    return jnp.dot(left, right, preferred_element_type=F32)


def dot_last(left, right):
    return lax.dot_general(left, right, (((1,), (1,)), ((), ())), preferred_element_type=F32)


def dot_first(left, right):
    return lax.dot_general(left, right, (((0,), (0,)), ((), ())), preferred_element_type=F32)


SIZES = (48, 32, 48,)
STARTS = tuple(sum(SIZES[:r]) for r in range(len(SIZES)))
ROUNDS = len(SIZES)

ORDER = (
    (0, 0, 0), (16,), (1, 0, 0, 3), (2, 0, 0, 1, 0), (1, 0, 0, 1), (2, 0, 0, 0, 0), (1, 0, 0, 2), (0, 0, 1),
    (2, 0, 0, 0, 3), (2, 0, 0, 1, 3), (2, 0, 0, 1, 1), (2, 0, 0, 0, 1), (3, 0, 0, 0), (1, 0, 1, 3),
    (2, 0, 0, 1, 2), (1, 0, 1, 1), (2, 0, 0, 0, 2), (2, 0, 1, 1, 0), (2, 0, 1, 0, 0), (3, 0, 0, 3),
    (1, 0, 1, 2), (0, 0, 2), (3, 0, 0, 1), (2, 0, 1, 1, 3), (2, 0, 1, 0, 3), (2, 0, 1, 0, 1), (3, 0, 0, 2),
    (3, 0, 1, 0), (2, 0, 1, 1, 1), (4, 0, 0), (5, 0, 0, 0, 0), (5, 1, 0, 0, 0), (2, 0, 1, 1, 2),
    (5, 1, 0, 0, 1), (2, 0, 1, 0, 2), (5, 0, 0, 0, 1), (1, 0, 2, 3), (2, 0, 2, 1, 0), (1, 0, 2, 1),
    (3, 0, 1, 3), (2, 0, 2, 0, 0), (3, 0, 1, 1), (1, 0, 2, 2), (0, 1, 0), (5, 0, 0, 1, 0), (3, 0, 1, 2),
    (5, 1, 0, 1, 0), (5, 1, 0, 1, 1), (2, 0, 2, 1, 3), (2, 0, 2, 0, 3), (5, 0, 0, 1, 1), (4, 0, 1),
    (5, 1, 1, 0, 1), (2, 0, 2, 0, 1), (2, 0, 2, 1, 1), (5, 1, 1, 0, 0), (5, 0, 1, 0, 1), (3, 0, 2, 0),
    (5, 0, 1, 0, 0), (5, 0, 0, 2, 0), (2, 0, 2, 1, 2), (1, 1, 0, 3), (5, 1, 0, 2, 0), (2, 1, 0, 1, 0),
    (2, 0, 2, 0, 2), (1, 1, 0, 1), (5, 1, 0, 2, 1), (3, 0, 2, 3), (2, 1, 0, 0, 0), (5, 0, 0, 2, 1),
    (5, 1, 1, 1, 0), (5, 1, 1, 1, 1), (3, 0, 2, 1), (1, 1, 0, 2), (0, 1, 1), (5, 0, 1, 1, 0), (5, 0, 1, 1, 1),
    (3, 0, 2, 2), (5, 0, 0, 3, 0), (2, 1, 0, 0, 3), (2, 1, 0, 1, 3), (2, 1, 0, 0, 1), (5, 1, 0, 3, 0),
    (4, 0, 2), (2, 1, 0, 1, 1), (5, 0, 2, 0, 0), (3, 1, 0, 0), (5, 0, 2, 0, 1), (5, 1, 1, 2, 0),
    (5, 1, 2, 0, 0), (5, 1, 2, 0, 1), (5, 0, 1, 2, 0), (1, 1, 1, 3), (5, 1, 1, 2, 1), (2, 1, 0, 1, 2),
    (1, 1, 1, 1), (2, 1, 1, 1, 0), (2, 1, 0, 0, 2), (5, 0, 1, 2, 1), (2, 1, 1, 0, 0), (3, 1, 0, 3), (6, 0),
    (1, 1, 1, 2), (0, 1, 2), (3, 1, 0, 1), (9, 0, 0, 0, 0), (5, 0, 2, 1, 1), (5, 1, 1, 3, 0), (5, 0, 2, 1, 0),
    (2, 1, 1, 1, 3), (2, 1, 1, 0, 3), (5, 1, 2, 1, 1), (2, 1, 1, 0, 1), (5, 1, 2, 1, 0), (3, 1, 0, 2),
    (3, 1, 1, 0), (2, 1, 1, 1, 1), (5, 0, 1, 3, 0), (4, 1, 0), (5, 2, 0, 0, 1), (8, 0, 0, 1, 0),
    (5, 2, 0, 0, 0), (2, 1, 1, 1, 2), (9, 0, 0, 1, 0), (1, 1, 2, 3), (2, 1, 1, 0, 2), (8, 0, 0, 1, 1),
    (9, 0, 0, 1, 1), (1, 1, 2, 1), (2, 1, 2, 1, 0), (3, 1, 1, 3), (2, 1, 2, 0, 0), (5, 0, 2, 2, 1),
    (3, 1, 1, 1), (5, 0, 2, 2, 0), (1, 1, 2, 2), (5, 1, 2, 2, 1), (5, 1, 2, 2, 0), (6, 1), (3, 1, 1, 2),
    (5, 2, 0, 1, 1), (2, 1, 2, 1, 3), (2, 1, 2, 0, 3), (9, 0, 1, 0, 0), (8, 0, 0, 2, 1), (9, 0, 0, 2, 1),
    (2, 1, 2, 0, 1), (8, 0, 0, 2, 0), (4, 1, 1), (3, 1, 2, 0), (5, 2, 0, 1, 0), (2, 1, 2, 1, 1),
    (2, 1, 2, 1, 2), (9, 0, 0, 2, 0), (2, 1, 2, 0, 2), (5, 2, 1, 0, 1), (5, 2, 1, 0, 0), (5, 0, 2, 3, 0),
    (8, 0, 1, 1, 1), (9, 0, 1, 1, 1), (5, 1, 2, 3, 0), (3, 1, 2, 3), (8, 0, 1, 1, 0), (9, 0, 1, 1, 0),
    (5, 2, 0, 2, 1), (3, 1, 2, 1), (3, 1, 2, 2), (8, 0, 0, 3, 0), (9, 0, 0, 3, 0), (8, 0, 0, 3, 1),
    (9, 0, 0, 3, 1), (5, 2, 1, 1, 1), (4, 1, 2), (5, 2, 0, 2, 0), (5, 2, 2, 0, 0), (8, 0, 1, 2, 1),
    (5, 2, 1, 1, 0), (9, 0, 1, 2, 1), (5, 2, 2, 0, 1), (6, 2), (8, 0, 1, 2, 0), (9, 0, 1, 2, 0),
    (5, 2, 1, 2, 1), (9, 0, 2, 0, 0), (8, 0, 0, 4, 0), (9, 0, 0, 4, 0), (8, 0, 1, 3, 1), (9, 0, 1, 3, 1),
    (5, 2, 0, 3, 0), (5, 2, 2, 1, 1), (5, 2, 2, 1, 0), (10, 0, 0), (11, 0, 0, 1), (11, 0, 0, 2), (11, 0, 0, 3),
    (11, 0, 0, 0), (12, 0, 0, 1, 0), (12, 0, 0, 1, 1), (12, 0, 0, 0, 2), (12, 0, 0, 0, 3), (5, 2, 1, 2, 0),
    (8, 0, 2, 1, 1), (9, 0, 2, 1, 1), (8, 0, 2, 1, 0), (9, 0, 2, 1, 0), (8, 0, 1, 3, 0), (9, 0, 1, 3, 0),
    (7, 0), (9, 1, 0, 0, 0), (12, 0, 0, 0, 1), (12, 0, 0, 1, 2), (5, 2, 2, 2, 0), (5, 2, 2, 2, 1),
    (12, 0, 0, 1, 3), (12, 0, 0, 0, 0), (5, 2, 1, 3, 0), (8, 0, 2, 2, 1), (9, 0, 2, 2, 1), (8, 0, 1, 4, 0),
    (9, 0, 1, 4, 0), (8, 0, 2, 2, 0), (9, 0, 2, 2, 0), (8, 1, 0, 1, 1), (8, 1, 0, 1, 0), (10, 0, 1),
    (11, 0, 1, 0), (11, 0, 1, 2), (11, 0, 1, 1), (11, 0, 1, 3), (12, 0, 1, 1, 1), (12, 0, 1, 1, 0),
    (13, 0, 0, 1), (13, 0, 0, 2), (12, 0, 1, 0, 3), (12, 0, 1, 0, 2), (8, 2, 0, 1, 0), (9, 1, 0, 1, 0),
    (13, 0, 0, 3), (13, 0, 0, 0), (8, 2, 0, 1, 1), (9, 1, 0, 1, 1), (5, 2, 2, 3, 0), (7, 1), (9, 1, 1, 0, 0),
    (12, 0, 1, 1, 2), (12, 0, 1, 0, 0), (8, 0, 2, 3, 1), (9, 0, 2, 3, 1), (8, 1, 0, 2, 1), (12, 0, 1, 1, 3),
    (12, 0, 1, 0, 1), (8, 0, 2, 3, 0), (9, 0, 2, 3, 0), (8, 1, 0, 2, 0), (8, 2, 0, 2, 1), (9, 1, 0, 2, 1),
    (8, 2, 0, 2, 0), (9, 1, 0, 2, 0), (8, 1, 1, 1, 1), (7, 2), (14, 0, 0), (8, 1, 1, 1, 0), (8, 2, 1, 1, 1),
    (13, 0, 1, 2), (13, 0, 1, 0), (9, 1, 1, 1, 1), (8, 2, 1, 1, 0), (13, 0, 1, 1), (13, 0, 1, 3),
    (8, 1, 0, 3, 1), (9, 1, 1, 1, 0), (9, 1, 2, 0, 0), (8, 2, 0, 3, 1), (9, 1, 0, 3, 1), (8, 0, 2, 4, 0),
    (8, 1, 1, 2, 1), (9, 0, 2, 4, 0), (8, 1, 0, 3, 0), (15, 2), (8, 2, 0, 3, 0), (9, 1, 0, 3, 0), (14, 0, 1),
    (8, 1, 2, 1, 1), (8, 1, 2, 1, 0), (10, 0, 2), (11, 0, 2, 0), (11, 0, 2, 2), (8, 2, 1, 2, 1),
    (9, 1, 1, 2, 1), (11, 0, 2, 3), (8, 1, 1, 3, 1), (11, 0, 2, 1), (12, 0, 2, 1, 0), (12, 0, 2, 0, 3),
    (8, 1, 1, 2, 0), (12, 0, 2, 0, 2), (12, 0, 2, 1, 1), (8, 2, 2, 1, 0), (9, 1, 2, 1, 0), (8, 2, 1, 2, 0),
    (8, 1, 0, 4, 0), (9, 1, 1, 2, 0), (8, 2, 2, 1, 1), (9, 1, 2, 1, 1), (8, 2, 0, 4, 0), (9, 1, 0, 4, 0),
    (8, 1, 2, 2, 1), (8, 1, 2, 2, 0), (12, 0, 2, 0, 0), (12, 0, 2, 1, 2), (8, 2, 1, 3, 1), (9, 1, 1, 3, 1),
    (8, 1, 1, 3, 0), (12, 0, 2, 1, 3), (12, 0, 2, 0, 1), (8, 2, 2, 2, 0), (9, 1, 2, 2, 0), (10, 1, 0),
    (11, 1, 0, 1), (11, 1, 0, 3), (11, 1, 0, 0), (11, 1, 0, 2), (12, 1, 0, 0, 2), (12, 1, 0, 1, 1),
    (12, 1, 0, 1, 0), (12, 1, 0, 0, 3), (8, 2, 1, 3, 0), (9, 1, 1, 3, 0), (8, 2, 2, 2, 1), (9, 1, 2, 2, 1),
    (8, 1, 2, 3, 1), (8, 1, 2, 3, 0), (13, 0, 2, 0), (8, 1, 1, 4, 0), (13, 0, 2, 2), (8, 2, 2, 3, 0),
    (9, 1, 2, 3, 0), (13, 0, 2, 1), (13, 0, 2, 3), (8, 2, 1, 4, 0), (9, 1, 1, 4, 0), (12, 1, 0, 1, 3),
    (12, 1, 0, 0, 1), (12, 1, 0, 0, 0), (12, 1, 0, 1, 2), (8, 2, 2, 3, 1), (9, 1, 2, 3, 1), (8, 1, 2, 4, 0),
    (10, 1, 1), (11, 1, 1, 1), (11, 1, 1, 0), (11, 1, 1, 2), (11, 1, 1, 3), (12, 1, 1, 0, 3), (12, 1, 1, 1, 1),
    (12, 1, 1, 1, 0), (12, 1, 1, 0, 2), (8, 2, 2, 4, 0), (9, 1, 2, 4, 0), (13, 1, 0, 3), (14, 0, 2),
    (10, 1, 2), (11, 1, 2, 0), (11, 1, 2, 2), (11, 1, 2, 1), (13, 1, 0, 1), (13, 1, 0, 2), (11, 1, 2, 3),
    (12, 1, 2, 0, 3), (12, 1, 2, 0, 2), (12, 1, 2, 1, 1), (13, 1, 0, 0), (12, 1, 2, 1, 0), (12, 1, 1, 1, 2),
    (12, 1, 1, 0, 1), (12, 1, 1, 1, 3), (12, 1, 1, 0, 0), (12, 1, 2, 1, 2), (12, 1, 2, 0, 0), (15, 0),
    (12, 1, 2, 0, 1), (12, 1, 2, 1, 3), (15, 1), (13, 1, 1, 2), (13, 1, 1, 3), (14, 1, 0), (13, 1, 2, 2),
    (13, 1, 1, 1), (13, 1, 1, 0), (13, 1, 2, 0), (13, 1, 2, 1), (13, 1, 2, 3), (14, 1, 1), (14, 1, 2),
)


def kernel(
    tok, wg, wu, wd, grd,
    out_ref, tg_ref, dg_ref, du_ref, dd_ref,
    act, w, rs_send, rs_recv, hall, gu, q, ps, pr, sa, ra, sb, rb, sc, rc,
    dw, outs, local_sem, out_sem, sent, r1, r2, r3, rp, zr, ar, prs, ras, rbs, rcs,
):
    c = lax.axis_index("gx")
    gy = lax.axis_index("gy")
    z = lax.axis_index("gz")
    y, x = gy // 4, gy % 4
    f = x * (1 - c) + y * c
    s = y * (1 - c) + x * c
    fm, sm = 1 + 3 * c, 4 - 3 * c
    sg = 1 - 2 * c
    partner = (1 - c, gy, z)

    def gy_of(f_, s_):
        return ((f_ + 8) % 4) * fm + ((s_ + 8) % 4) * sm

    def at_fs(f_, s_):
        return (c, gy_of(f_, s_), z)

    def mod8(k):
        return (k + 16) % 8

    def at_z(k):
        return (c, gy, mod8(z + k))

    def rows_of(r, block):
        return pl.ds(pl.multiple_of(16 * STARTS[r] + block * SIZES[r], 16), SIZES[r])

    def zrows(r, block):
        return pl.ds(pl.multiple_of(16 * STARTS[r] + block * 2 * SIZES[r], 16), 2 * SIZES[r])

    def round_rows(r):
        return pl.ds(16 * STARTS[r], 16 * SIZES[r])

    def cut(r):
        return pl.ds(STARTS[r], SIZES[r])

    def zcut(r):
        return pl.ds(2 * STARTS[r], 2 * SIZES[r])

    def send(src, dst, family, rs, device):
        pltpu.make_async_remote_copy(
            src_ref=src, dst_ref=dst, send_sem=sent.at[family], recv_sem=rs,
            device_id=device, device_id_type=MESH,
        ).start()

    def recv(dst, rs):
        pltpu.make_async_remote_copy(
            src_ref=dst, dst_ref=dst, send_sem=sent.at[0], recv_sem=rs,
            device_id=partner, device_id_type=MESH,
        ).wait_recv()

    def all_sent(family, ref):
        pltpu.make_async_remote_copy(
            src_ref=ref, dst_ref=ref, send_sem=sent.at[family], recv_sem=local_sem.at[0],
            device_id=partner, device_id_type=MESH,
        ).wait_send()

    barrier = pltpu.get_barrier_semaphore()
    peers = [
        at_fs(f + 1, s), at_fs(f + 2, s), at_fs(f + 3, s), at_fs(f, s + 1), at_fs(f, s + 3),
        at_z(1), at_z(-1), partner,
    ]
    for peer in peers:
        pl.semaphore_signal(barrier, inc=1, device_id=peer, device_id_type=MESH)

    own = (tok, grd)

    def own_rows(a, r):
        return own[a].at[cut(r)]

    locals_ = [
        pltpu.make_async_copy(ref, w.at[k], local_sem.at[k]) for k, ref in enumerate((wg, wu, wd))
    ] + [
        pltpu.make_async_copy(
            own_rows(a, r), act.at[a, c, rows_of(r, gy)], local_sem.at[3 + 2 * r + a]
        )
        for r in range(ROUNDS) for a in range(2)
    ]
    for copy in locals_[3:] + locals_[:3]:
        copy.start()
    pl.semaphore_wait(barrier, len(peers))

    def act_block(a, r, k, t):
        return act.at[a, c, rows_of(r, gy_of(f - k, s + t))]

    def to_partner(a, r, k, t, src=None):
        ref = act_block(a, r, k, t)
        send(
            ref if src is None else src, ref,
            3, rp.at[a, r], partner,
        )

    def gather_own(a, r):
        ref = src = act_block(a, r, 0, 0)
        locals_[3 + 2 * r + a].wait()
        for k in (1, 3, 2):
            send(src, ref, 0, r1.at[a, r, k - 1], at_fs(f + k, s))
        send(src, ref, 1, r2.at[a, r, 0, 0], at_fs(f, s + 1))
        send(src, ref, 1, r2.at[a, r, 1, 0], at_fs(f, s + 3))
        to_partner(a, r, 0, 0, src)

    def gather_row(a, r, k):
        ref = act_block(a, r, k, 0)
        recv(ref, r1.at[a, r, k - 1])
        send(ref, ref, 1, r2.at[a, r, 0, k], at_fs(f, s + 1))
        send(ref, ref, 1, r2.at[a, r, 1, k], at_fs(f, s + 3))
        to_partner(a, r, k, 0)

    def gather_near(a, r, way, k):
        t = (3, 1)[way]
        ref = act_block(a, r, k, t)
        recv(ref, r2.at[a, r, way, k])
        if (way == 0) == (k < 2):
            send(ref, ref, 2, r3.at[a, r, k], at_fs(f, s + 1 + 2 * way))
        to_partner(a, r, k, t)

    def gather_far(a, r, k):
        ref = act_block(a, r, k, 2)
        recv(ref, r3.at[a, r, k])
        to_partner(a, r, k, 2)

    def gather_end(a, r):
        recv(act.at[a, 1 - c, round_rows(r)], rp.at[a, r])

    def part(a, r, d):
        rows = zrows(r, d)
        source = 0 if a < 2 else 1
        return dot_plain(act[source, 0, rows, :], w[a, 0:512, :]) + dot_plain(
            act[source, 1, rows, :], w[a, 512:1024, :]
        )

    def sum_recv(a, r, slot):
        recv(rs_recv.at[a, slot, zcut(r)], zr.at[a, r, slot])
        return rs_recv[a, slot, zcut(r), :].astype(F32)

    def sum_step(a, r, j, way):
        slot = 4 * way + j
        to = (-sg, sg)[way]
        value = part(a, r, mod8(z + to * (4 - way - j)))
        if j > 0:
            value = value + sum_recv(a, r, slot - 1)
        rs_send[a, slot, zcut(r), :] = value.astype(BF16)
        send(
            rs_send.at[a, slot, zcut(r)], rs_recv.at[a, slot, zcut(r)],
            4, zr.at[a, r, slot], at_z(to),
        )

    def sum_end(a, r):
        value = part(a, r, z)
        for slot in (3, 6):
            value = value + sum_recv(a, r, slot)
        return value

    def zgather(t, r, j, way):
        slot = 4 * way + j
        to = (-sg, sg)[way]
        ref = hall.at[t, zrows(r, mod8(z - to * j))]
        if j > 0:
            recv(ref, ar.at[t, r, slot - 1])
        if j < 4 - way:
            send(ref, ref, 5, ar.at[t, r, slot], at_z(to))

    def product(o, r, b, half):
        rows = zrows(r, b)
        cols = pl.ds(pl.multiple_of(half * 512, 512), 512)
        if o == 0:
            return dot_last(hall[0, rows, :], w[2, cols, :])
        return dot_last(hall[1, rows, :], w[0, cols, :]) + dot_last(hall[2, rows, :], w[1, cols, :])

    def out_block(o, r, j, way):
        b = mod8(z + (sg, -sg)[way] * j)
        rows = zrows(r, b)
        ps[o, rows, :] = product(o, r, b, 1 - c).astype(BF16)
        send(ps.at[o, rows], pr.at[o, rows], 6, prs.at[o, r], partner)
        q[o, rows, :] = product(o, r, b, c)

    def out_pair(o, r):
        recv(pr.at[o, round_rows(r)], prs.at[o, r])

    done = []

    def put(k, src, dst):
        copy = pltpu.make_async_copy(src, dst, out_sem.at[k])
        copy.start()
        done.append(copy)

    def chip_sum(o, r, k, t):
        rows = rows_of(r, gy_of(f + k, s + t))
        return q[o, rows, :] + pr[o, rows, :].astype(F32)

    def stage_a(o, r, k):
        sa[o, k, cut(r), :] = chip_sum(o, r, k, 2).astype(BF16)
        send(
            sa.at[o, k, cut(r)], ra.at[o, k, cut(r)], 7, ras.at[o, r, k],
            at_fs(f, s + (1 if k < 2 else 3)),
        )

    def stage_b(o, r, way, k):
        t = (1, 3)[way]
        value = chip_sum(o, r, k, t)
        if (way == 0) == (k < 2):
            recv(ra.at[o, k, cut(r)], ras.at[o, r, k])
            value = value + ra[o, k, cut(r), :].astype(F32)
        sb[o, k, way, cut(r), :] = value.astype(BF16)
        send(
            sb.at[o, k, way, cut(r)], rb.at[o, k, way, cut(r)],
            8, rbs.at[o, r, k], at_fs(f, s + t),
        )

    def stage_c(o, r, k):
        value = chip_sum(o, r, k, 0)
        recv(rb.at[o, k, :, cut(r)], rbs.at[o, r, k])
        for way in range(2):
            value = value + rb[o, k, way, cut(r), :].astype(F32)
        if k > 0:
            sc[o, k, cut(r), :] = value.astype(BF16)
            send(
                sc.at[o, k, cut(r)], rc.at[o, k, cut(r)], 9, rcs.at[o, r],
                at_fs(f + k, s),
            )
        else:
            q[o, rows_of(r, gy), :] = value

    def stage_d(o, r):
        value = q[o, rows_of(r, gy), :]
        recv(rc.at[o, pl.ds(1, 3), cut(r)], rcs.at[o, r])
        for k in (1, 3, 2):
            value = value + rc[o, k, cut(r), :].astype(F32)
        outs[o, cut(r), :] = value.astype(BF16)
        if r == ROUNDS - 1:
            put(o, outs.at[o], (out_ref, tg_ref)[o])

    def weight_grad(k):
        ref, a, t = ((dg_ref, 0, 1), (du_ref, 0, 2), (dd_ref, 1, 0))[k]
        for half in range(2):
            dw[k, half * 512:(half + 1) * 512, :] = dot_first(act[a, half], hall[t])
        put(2 + k, dw.at[k], ref)

    def forward(r):
        gate = sum_end(0, r)
        gu[0, zcut(r), :] = gate
        gated = gate * jax.nn.sigmoid(gate)
        up = sum_end(1, r)
        gu[1, zcut(r), :] = up
        hall[0, zrows(r, z), :] = (gated * up).astype(BF16)
        for way in range(2):
            zgather(0, r, 0, way)

    def backward(r):
        hidden_grad = sum_end(2, r)
        gate = gu[0, zcut(r), :]
        up = gu[1, zcut(r), :]
        sigmoid = jax.nn.sigmoid(gate)
        hall[1, zrows(r, z), :] = (
            hidden_grad * up * sigmoid * (1.0 + gate * (1.0 - sigmoid))
        ).astype(BF16)
        hall[2, zrows(r, z), :] = (hidden_grad * (gate * sigmoid)).astype(BF16)
        for t in (1, 2):
            for way in range(2):
                zgather(t, r, 0, way)

    def weights():
        for copy in locals_[:3]:
            copy.wait()

    phases = (
        gather_own, gather_row, gather_near, gather_far, gather_end, sum_step, forward, backward,
        zgather, out_block, out_pair, stage_a, stage_b, stage_c, stage_d, weight_grad, weights,
    )
    for kind, *rest in ORDER:
        phases[kind](*rest)
    for family, ref in enumerate((
        act.at[0, 0, pl.ds(0, 768)], act.at[0, 0], act.at[0, 0, pl.ds(0, 1024)], act.at[:, 0],
        rs_send, rs_send, ps, sa, sb, sc.at[:, pl.ds(1, 3)],
    )):
        all_sent(family, ref)
    for copy in done:
        copy.wait()


def put_out(*refs):
    sems = refs[10]
    copies = [pltpu.make_async_copy(refs[k], refs[5 + k], sems.at[k]) for k in range(2)] + [
        pltpu.make_async_copy(
            refs[k].at[pl.ds(256 * n, 256)], refs[5 + k].at[pl.ds(256 * n, 256)],
            sems.at[2 + 4 * (k - 2) + n],
        )
        for k in range(2, 5) for n in range(4)
    ]
    for copy in copies:
        copy.start()
    for copy in copies:
        copy.wait()


def per_device(tokens, gate_weight, up_weight, down_weight, out_grad):
    dma = pltpu.SemaphoreType.DMA
    vmem = pltpu.VMEM

    results = pl.pallas_call(
        kernel,
        out_shape=(
            pltpu.VMEM((128, 512), BF16),
            pltpu.VMEM((128, 512), BF16),
            pltpu.VMEM((1024, 256), F32),
            pltpu.VMEM((1024, 256), F32),
            pltpu.VMEM((1024, 256), F32),
        ),
        in_specs=[pl.BlockSpec(memory_space=pltpu.HBM)] * 5,
        out_specs=tuple([pl.BlockSpec(memory_space=pl.ANY)] * 5),
        scratch_shapes=[
            vmem((2, 2, 2048, 512), BF16),
            vmem((3, 1024, 256), BF16),
            vmem((3, 7, 256, 256), BF16),
            vmem((3, 7, 256, 256), BF16),
            vmem((3, 2048, 256), BF16),
            vmem((2, 256, 256), F32),
            vmem((2, 2048, 512), F32),
            vmem((2, 2048, 512), BF16),
            vmem((2, 2048, 512), BF16),
            vmem((2, 4, 128, 512), BF16),
            vmem((2, 4, 128, 512), BF16),
            vmem((2, 4, 2, 128, 512), BF16),
            vmem((2, 4, 2, 128, 512), BF16),
            vmem((2, 4, 128, 512), BF16),
            vmem((2, 4, 128, 512), BF16),
            vmem((3, 1024, 256), F32),
            vmem((2, 128, 512), BF16),
            dma((3 + 2 * ROUNDS,)),
            dma((5,)),
            dma((10,)),
            dma((2, ROUNDS, 3)),
            dma((2, ROUNDS, 2, 4)),
            dma((2, ROUNDS, 4)),
            dma((2, ROUNDS)),
            dma((3, ROUNDS, 7)),
            dma((3, ROUNDS, 7)),
            dma((2, ROUNDS)),
            dma((2, ROUNDS, 4)),
            dma((2, ROUNDS, 4)),
            dma((2, ROUNDS)),
        ],
        compiler_params=pltpu.CompilerParams(
            collective_id=0, has_side_effects=True, vmem_limit_bytes=56 * 1024 * 1024
        ),
        name="slab",
    )(tokens, gate_weight, up_weight, down_weight, out_grad)

    shapes = tuple(jax.ShapeDtypeStruct(value.shape, value.dtype) for value in results)
    return pl.pallas_call(
        put_out,
        out_shape=shapes,
        in_specs=[pl.BlockSpec(memory_space=pl.ANY)] * 5,
        out_specs=tuple([pl.BlockSpec(memory_space=pltpu.HBM)] * 5),
        scratch_shapes=[dma((14,))],
        compiler_params=pltpu.CompilerParams(vmem_limit_bytes=1024 * 1024),
        name="put_out",
    )(*results)


def solution(mesh):
    return jax.shard_map(
        per_device,
        mesh=mesh,
        in_specs=(
            P("gy", ("gz", "gx")),
            P("gz", ("gx", "gy")),
            P("gz", ("gx", "gy")),
            P("gz", ("gx", "gy")),
            P("gy", ("gz", "gx")),
        ),
        out_specs=(
            P("gy", ("gz", "gx")),
            P("gy", ("gz", "gx")),
            P("gz", ("gx", "gy")),
            P("gz", ("gx", "gy")),
            P("gz", ("gx", "gy")),
        ),
        check_vma=False,
    )
```
